32 devices in a mesh: shard: 2 (over x), ctx: 4 (over y, core), tp: 4 (over z).
Axes of the slice: x: 2, y: 2, z: 4, core: 2. Of those that a mesh axis runs over, the one named last changes fastest.
Arguments:
- tokens: bfloat16 [8, 1024, 767], P('shard', 'ctx'), may hold values from -6 to 6
- lengths: int32 [8], P('shard'), may hold values from 256 to 1024, as said below
- first_gain: float32 [768], replicated, may hold values from 0.5 to 1.5
- entry_weight: bfloat16 [3, 768, 768], P(None, ('shard', 'ctx'), 'tp'), may hold values from -0.21875 to 0.21875
- entry_bias: float32 [2, 768], P(None, 'tp'), may hold values from -3 to 3
- exit_weight: bfloat16 [768, 768], P('tp', ('shard', 'ctx')), may hold values from -0.625 to 0.625
- exit_bias: float32 [768], replicated, may hold values from -3 to 3
- second_gain: float32 [768], replicated, may hold values from 0.5 to 1.5
- hidden_weight: bfloat16 [768, 3072], P(('shard', 'ctx'), 'tp'), may hold values from -0.21875 to 0.21875
- hidden_bias: float32 [3072], P('tp'), may hold values from -3 to 3
- return_weight: bfloat16 [3072, 768], P('tp', ('shard', 'ctx')), may hold values from -0.109375 to 0.109375
- return_bias: float32 [768], replicated, may hold values from -3 to 3
- cotangent: bfloat16 [8, 1024, 767], P('shard', 'ctx'), may hold values from -6 to 6
Outputs:
- result: bfloat16 [8, 1024, 767], P('shard', 'ctx')
- tokens_gradient: bfloat16 [8, 1024, 767], P('shard', 'ctx')
- first_gain_gradient: float32 [768], replicated
- entry_weight_gradient: float32 [3, 768, 768], P(None, ('shard', 'ctx'), 'tp')
- entry_bias_gradient: float32 [2, 768], P(None, 'tp')
- exit_weight_gradient: float32 [768, 768], P('tp', ('shard', 'ctx'))
- exit_bias_gradient: float32 [768], replicated
- second_gain_gradient: float32 [768], replicated
- hidden_weight_gradient: float32 [768, 3072], P(('shard', 'ctx'), 'tp')
- hidden_bias_gradient: float32 [3072], P('tp')
- return_weight_gradient: float32 [3072, 768], P('tp', ('shard', 'ctx'))
- return_bias_gradient: float32 [768], replicated
The draws below stay inside these ranges and needn't reach their ends.
Inputs may be any that keep to these rules, and one draw needn't show every extreme that they name: `lengths`: in every draw some sequence has exactly 1024 valid positions and some has exactly 256.
All inputs are finite; a program needn't handle non-finite values.
Results may differ from the reference program's by a relative error of at most 0.014.
Values may be sent and summed in bfloat16 or wider, within the bound.
No kernel may reach another device: no remote copies, remote signals or barrier semaphores. Data moves between devices by JAX's collectives and lax.ppermute only.
A program may use at most 256 MiB of HBM per device.

```python
import math
import jax
import jax.numpy as jnp
from jax import lax

D = 768
HEADS = 12
HDIM = 64
FF = 3072
SEQ_DEV = 4
SEQ_LEN = 1024
SEQS = 8
DC = 767
N_SHARD = 2


def draw_lengths(key, part):
    key_values, key_first, key_step = jax.random.split(key, 3)
    shortest = SEQ_LEN // 4
    drawn = jax.random.randint(key_values, (SEQS,), shortest, SEQ_LEN + 1)
    first_slot = jax.random.randint(key_first, (), 0, SEQS)
    offset_slot = jax.random.randint(key_step, (), 1, SEQS)
    second_slot = (first_slot + offset_slot) % SEQS
    indices = jnp.arange(SEQS)
    drawn = jnp.where(indices == first_slot, SEQ_LEN, drawn)
    drawn = jnp.where(indices == second_slot, shortest, drawn)
    return drawn.astype(jnp.int32)


def levels(own_key, dims, cuts, smallest, largest):
    level, own = 1.0, jax.random.fold_in(own_key, 6)
    for axis_at, parts in cuts:
        draws = jnp.exp(jax.random.uniform(jax.random.fold_in(own, axis_at), (parts,), jnp.float32, smallest / len(cuts), largest / len(cuts)))
        level = level * jnp.repeat(draws, dims[axis_at] // parts).reshape([-1 if axis == axis_at else 1 for axis in range(len(dims))])
    return level


def normal_values(key, extent, scale, reach, cuts=(), kind=jnp.bfloat16):
    values = scale * jax.random.normal(key, extent, jnp.float32)
    if cuts:
        values = values * levels(key, extent, cuts, -0.22, 0.18)
    return jnp.clip(values, -reach, reach).astype(kind)


def setup_inputs(seed: int = 0) -> dict:
    seeds = jax.random.split(jax.random.key(seed), 14)
    return {
        "tokens": normal_values(seeds[0], (SEQS, SEQ_LEN, DC), 1.0, 6.0, ((0, 2), (1, 4))),
        "lengths": draw_lengths(jax.random.fold_in(seeds[13], 71), 0),
        "first_gain": jnp.clip(1.0 + 0.1 * jax.random.normal(seeds[2], (D,), jnp.float32), 0.5, 1.5),
        "entry_weight": normal_values(seeds[3], (3, D, D), D ** -0.5, 0.21875, ((1, 8), (2, 4))),
        "entry_bias": normal_values(seeds[4], (2, D), 0.5, 3.0, ((1, 4),), jnp.float32),
        "exit_weight": normal_values(seeds[5], (D, D), (D // 8) ** -0.5, 0.625, ((0, 4), (1, 8))),
        "exit_bias": normal_values(seeds[6], (D,), 0.5, 3.0, (), jnp.float32),
        "second_gain": jnp.clip(1.0 + 0.1 * jax.random.normal(seeds[7], (D,), jnp.float32), 0.5, 1.5),
        "hidden_weight": normal_values(seeds[8], (D, FF), D ** -0.5, 0.21875, ((0, 8), (1, 4))),
        "hidden_bias": normal_values(seeds[9], (FF,), 0.5, 3.0, ((0, 4),), jnp.float32),
        "return_weight": normal_values(seeds[10], (FF, D), FF ** -0.5, 0.109375, ((0, 4), (1, 8))),
        "return_bias": normal_values(seeds[11], (D,), 0.5, 3.0, (), jnp.float32),
        "cotangent": normal_values(seeds[12], (SEQS, SEQ_LEN, DC), 1.0, 6.0, ((0, 2), (1, 4))),
    }


EPSILON = 1e-05

@jax.custom_vjp
def low(v):
    return lax.optimization_barrier(v.astype(jnp.bfloat16)).astype(jnp.float32)

@jax.custom_vjp
def low_back(v):
    return v

def low_keep(v):
    return (low(v), None)

def low_pass(kept, grad):
    return (grad,)

def back_keep(v):
    return (v, None)

def back_low(kept, grad):
    return (low(grad),)
low.defvjp(low_keep, low_pass)
low_back.defvjp(back_keep, back_low)

def attend_one(operands):
    queries, keys, values, length = operands
    highest = lax.Precision.HIGHEST
    raw_scores = jnp.einsum('qhd,khd->hqk', queries, keys, precision=highest)
    scaled = low_back(raw_scores * (1.0 / math.sqrt(HDIM)))
    positions = jnp.arange(SEQ_LEN, dtype=jnp.int32)
    allowed = (positions[None, :] <= positions[:, None]) & (positions[None, :] < length)
    masked = jnp.where(allowed[None], scaled, -1e+30)
    weights = low_back(low(jax.nn.softmax(masked, axis=-1)))
    return jnp.einsum('hqk,khd->qhd', weights, values, precision=highest)

def center(values):
    return values - lax.optimization_barrier(jnp.mean(values, -1, keepdims=True))

def normalize(values, gain_values):
    return values * lax.rsqrt(lax.optimization_barrier(jnp.mean(values * values, -1, keepdims=True)) + EPSILON) * gain_values

def forward(compressed, lengths, first_gain, entry_weight, entry_bias, exit_weight, exit_bias, second_gain, hidden_weight, hidden_bias, return_weight, return_bias):
    highest = lax.Precision.HIGHEST
    groups = compressed.shape[0]
    stream = jnp.concatenate([compressed, -lax.optimization_barrier(jnp.sum(compressed, -1, keepdims=True))], -1)
    normed = low(normalize(stream, first_gain))
    queries = low_back(low(jnp.einsum('gld,de->gle', normed, entry_weight[0], precision=highest) + entry_bias[0]))
    keys = low_back(low(jnp.einsum('gld,de->gle', normed, entry_weight[1], precision=highest)))
    values = low_back(low(jnp.einsum('gld,de->gle', normed, entry_weight[2], precision=highest) + entry_bias[1]))
    shaped = (groups, SEQ_LEN, HEADS, HDIM)
    attended = lax.map(jax.checkpoint(attend_one), (queries.reshape(shaped), keys.reshape(shaped), values.reshape(shaped), lengths))
    attended = low_back(low(attended.reshape(groups, SEQ_LEN, D)))
    branch = low_back(jnp.einsum('gle,ed->gld', attended, exit_weight, precision=highest) + exit_bias)
    middle = stream + center(branch)
    normed_second = low(normalize(middle, second_gain))
    hidden = low_back(jnp.einsum('gld,df->glf', normed_second, hidden_weight, precision=highest) + hidden_bias)
    activated = low(jax.nn.gelu(hidden, approximate=True))
    returned = low_back(jnp.einsum('glf,fd->gld', activated, return_weight, precision=highest) + return_bias)
    full_stream = middle + center(returned)
    return full_stream[..., :DC]

def reference(tokens, lengths, first_gain, entry_weight, entry_bias, exit_weight, exit_bias, second_gain, hidden_weight, hidden_bias, return_weight, return_bias, cotangent):
    params = tuple((entry.astype(jnp.float32) for entry in (first_gain, entry_weight, entry_bias, exit_weight, exit_bias, second_gain, hidden_weight, hidden_bias, return_weight, return_bias)))
    stacked_tokens = tokens.astype(jnp.float32).reshape(N_SHARD, SEQ_DEV, SEQ_LEN, DC)
    stacked_lengths = lengths.reshape(N_SHARD, SEQ_DEV)
    stacked_cot = cotangent.astype(jnp.float32).reshape(N_SHARD, SEQ_DEV, SEQ_LEN, DC)
    positions = jnp.arange(SEQ_LEN, dtype=jnp.int32)

    def step(running, item):
        group_tokens, group_lengths, group_cot = item
        valid = (positions[None, :] < group_lengths[:, None]).astype(jnp.float32)

        def apply(stream_in, *weights):
            return forward(stream_in, group_lengths, *weights)
        outputs, pullback = jax.vjp(apply, group_tokens, *params)
        gradients = pullback(group_cot * valid[..., None])
        running = tuple((total + gradient for total, gradient in zip(running, gradients[1:])))
        return (running, (outputs.astype(jnp.bfloat16), gradients[0].astype(jnp.bfloat16)))
    zeroes = tuple((jnp.zeros_like(entry) for entry in params))
    running, (outputs, input_grads) = lax.scan(step, zeroes, (stacked_tokens, stacked_lengths, stacked_cot))
    return (outputs.reshape(SEQS, SEQ_LEN, DC), input_grads.reshape(SEQS, SEQ_LEN, DC), running[0], running[1], running[2], running[3], running[4], running[5], running[6], running[7], running[8], running[9])
```

```python
import functools
import math

import jax
import jax.numpy as jnp
from jax import lax
from jax.experimental import pallas as pl
from jax.experimental.pallas import tpu as pltpu
from jax.sharding import PartitionSpec as P

HDIM = 64
PAIR = 2 * HDIM
EPSILON = 1e-05
MASKED = -1e30
LOW = jnp.bfloat16
SINGLE = jnp.float32


def row_mean(values):
    return jnp.mean(values, -1, keepdims=True)


def dot(left, right):
    return jnp.dot(left, right, preferred_element_type=SINGLE)


def dot_nt(left, right):
    return lax.dot_general(left, right, (((1,), (1,)), ((), ())), preferred_element_type=SINGLE)


def dot_tn(left, right):
    return lax.dot_general(left, right, (((0,), (0,)), ((), ())), preferred_element_type=SINGLE)


def key_positions(meta, block, local, upper):
    base = upper * 2 * local + (meta[1] ^ block) * local
    return base + lax.broadcasted_iota(jnp.int32, (local, 1), 0)


def query_positions(meta, block, local):
    base = meta[0] * 2 * local + (meta[1] ^ block) * local
    return base + lax.broadcasted_iota(jnp.int32, (1, local), 1)


def masks(meta, block, local):
    near_pos = jnp.concatenate([key_positions(meta, b, local, meta[0]) for b in (0, 1)], 0)
    far_pos = jnp.concatenate([key_positions(meta, b, local, 0) for b in (0, 1)], 0)
    near = (near_pos <= query_positions(meta, block, local)) & (near_pos < meta[2])
    far = far_pos < jnp.where(meta[0] == 1, meta[2], 0)
    return near, far


def half_of(values, head):
    lanes = lax.broadcasted_iota(jnp.int32, values.shape, 1)
    return jnp.where((lanes >= HDIM) == (head == 1), values, jnp.zeros_like(values))


def forward_kernel(meta, q_ref, k_ref, v_ref, kf_ref, vf_ref, out_ref, log_ref):
    local = q_ref.shape[0] // 2
    scale = 1.0 / math.sqrt(HDIM)
    for block in (0, 1):
        near, far = masks(meta, block, local)
        rows = pl.ds(block * local, local)
        parts = []
        for head in (0, 1):
            query = half_of(q_ref[rows, :], head) * jnp.asarray(scale, LOW)
            near_s = jnp.where(near, dot_nt(k_ref[...], query), MASKED)
            far_s = jnp.where(far, dot_nt(kf_ref[...], query), MASKED)
            top = jnp.maximum(
                jnp.max(near_s, 0, keepdims=True), jnp.max(far_s, 0, keepdims=True)
            )
            near_p = jnp.exp(near_s - top)
            far_p = jnp.exp(far_s - top)
            total = jnp.sum(near_p, 0, keepdims=True) + jnp.sum(far_p, 0, keepdims=True)
            mixed = dot_tn(v_ref[...], near_p.astype(LOW)) + dot_tn(vf_ref[...], far_p.astype(LOW))
            parts.append(mixed[head * HDIM : (head + 1) * HDIM] / total)
            log_ref[0, head : head + 1, rows] = top + jnp.log(total)
        out_ref[rows, :] = jnp.concatenate(parts, 0).T.astype(LOW)


def attention_forward(meta, queries, near_kv, far_kv):
    rows, width = queries.shape
    pairs = width // PAIR
    block = functools.partial(pl.BlockSpec, (rows, PAIR))
    return pl.pallas_call(
        forward_kernel,
        grid_spec=pltpu.PrefetchScalarGridSpec(
            num_scalar_prefetch=1,
            grid=(pairs,),
            in_specs=[
                block(lambda j, meta: (0, j)),
                block(lambda j, meta: (0, j)),
                block(lambda j, meta: (0, pairs + j)),
                block(lambda j, meta: (0, j)),
                block(lambda j, meta: (0, pairs + j)),
            ],
            out_specs=[
                block(lambda j, meta: (0, j)),
                pl.BlockSpec((1, 2, rows), lambda j, meta: (j, 0, 0)),
            ],
        ),
        out_shape=[
            jax.ShapeDtypeStruct((rows, width), LOW),
            jax.ShapeDtypeStruct((pairs, 2, rows), SINGLE),
        ],
        cost_estimate=pl.CostEstimate(
            flops=8 * rows * rows * width * 2, bytes_accessed=rows * width * 14,
            transcendentals=2 * rows * rows * width // HDIM,
        ),
        name="attend",
    )(meta, queries, near_kv, near_kv, far_kv, far_kv)


def backward_kernel(
    meta, q_ref, k_ref, v_ref, kf_ref, vf_ref, grad_ref, log_ref,
    dq_ref, dk_ref, dv_ref, dkf_ref, dvf_ref, sums
):
    local = q_ref.shape[0] // 2
    scale = 1.0 / math.sqrt(HDIM)
    for block in (0, 1):
        near, far = masks(meta, block, local)
        rows = pl.ds(block * local, local)
        parts = []
        for head in (0, 1):
            query = half_of(q_ref[rows, :], head) * jnp.asarray(scale, LOW)
            out_grad = half_of(grad_ref[rows, :], head)
            log_total = log_ref[0, head : head + 1, rows]
            near_p = jnp.exp(jnp.where(near, dot_nt(k_ref[...], query), MASKED) - log_total)
            far_p = jnp.exp(jnp.where(far, dot_nt(kf_ref[...], query), MASKED) - log_total)
            near_g = dot_nt(v_ref[...], out_grad).astype(LOW).astype(SINGLE)
            far_g = dot_nt(vf_ref[...], out_grad).astype(LOW).astype(SINGLE)
            inner = jnp.sum(near_p * near_g, 0, keepdims=True) + jnp.sum(
                far_p * far_g, 0, keepdims=True
            )
            near_d = (near_p * (near_g - inner)).astype(LOW)
            far_d = (far_p * (far_g - inner)).astype(LOW)
            fresh = (
                dot(near_d, query), dot(near_p.astype(LOW), out_grad),
                dot(far_d, query), dot(far_p.astype(LOW), out_grad),
            )
            for at, value in enumerate(fresh):
                if block == 0 and head == 0:
                    sums[at] = value
                else:
                    sums[at] = sums[at] + value
            mixed = dot_tn(k_ref[...], near_d) + dot_tn(kf_ref[...], far_d)
            parts.append(mixed[head * HDIM : (head + 1) * HDIM] * scale)
        dq_ref[rows, :] = jnp.concatenate(parts, 0).T.astype(LOW)
    dk_ref[...] = sums[0]
    dv_ref[...] = sums[1]
    dkf_ref[...] = sums[2].astype(LOW)
    dvf_ref[...] = sums[3].astype(LOW)


def attention_backward(meta, queries, near_kv, far_kv, grads, logs):
    rows, width = queries.shape
    pairs = width // PAIR
    block = functools.partial(pl.BlockSpec, (rows, PAIR))
    same = lambda j, meta: (0, j)
    return pl.pallas_call(
        backward_kernel,
        grid_spec=pltpu.PrefetchScalarGridSpec(
            num_scalar_prefetch=1,
            grid=(pairs,),
            in_specs=[
                block(same),
                block(same),
                block(lambda j, meta: (0, pairs + j)),
                block(same),
                block(lambda j, meta: (0, pairs + j)),
                block(same),
                pl.BlockSpec((1, 2, rows), lambda j, meta: (j, 0, 0)),
            ],
            out_specs=[block(same)] * 5,
            scratch_shapes=[pltpu.VMEM((4, rows, PAIR), SINGLE)],
        ),
        out_shape=[
            jax.ShapeDtypeStruct((rows, width), LOW),
            jax.ShapeDtypeStruct((rows, width), SINGLE),
            jax.ShapeDtypeStruct((rows, width), SINGLE),
            jax.ShapeDtypeStruct((rows, width), LOW),
            jax.ShapeDtypeStruct((rows, width), LOW),
        ],
        cost_estimate=pl.CostEstimate(
            flops=20 * rows * rows * width * 2, bytes_accessed=rows * width * 30,
            transcendentals=2 * rows * rows * width // HDIM,
        ),
        name="attend_back",
    )(meta, queries, near_kv, near_kv, far_kv, far_kv, grads, logs)


class Place:
    def __init__(self):
        self.n_shard = lax.axis_size("shard")
        self.n_ctx = lax.axis_size("ctx")
        self.n_tp = lax.axis_size("tp")
        self.shard = lax.axis_index("shard")
        ctx = lax.axis_index("ctx")
        self.ctx = ctx
        self.half = ctx // 2
        self.core = ctx % 2
        self.tp = lax.axis_index("tp")
        self.home = self.core == self.tp // 2

    def core_swap(self, value):
        return lax.ppermute(value, "ctx", [(i, i ^ 1) for i in range(self.n_ctx)])

    def half_swap(self, value):
        return lax.ppermute(value, "ctx", [(i, i ^ 2) for i in range(self.n_ctx)])

    def half_up(self, value):
        return lax.ppermute(value, "ctx", [(0, 2), (1, 3)])

    def half_down(self, value):
        return lax.ppermute(value, "ctx", [(2, 0), (3, 1)])

    def shard_swap(self, value):
        return lax.ppermute(value, "shard", [(0, 1), (1, 0)])

    def tp_swap(self, value, mask):
        return lax.ppermute(value, "tp", [(i, i ^ mask) for i in range(self.n_tp)])

    def mixed(self, value, pairs):
        flat = [(a * self.n_tp + b, c * self.n_tp + d) for (a, b), (c, d) in pairs]
        return lax.ppermute(value, ("ctx", "tp"), flat)

    def to_home(self, value):
        return self.mixed(
            value,
            [((2 * h + 1 - z // 2, z), (2 * h + z // 2, z)) for h in (0, 1) for z in range(4)],
        )

    def from_home(self, value):
        return self.mixed(
            value,
            [((2 * h + z // 2, z), (2 * h + 1 - z // 2, z)) for h in (0, 1) for z in range(4)],
        )

    def spread(self, value, mask):
        return self.mixed(
            value,
            [((2 * h + z // 2, z), (2 * h + z // 2, z ^ mask)) for h in (0, 1) for z in range(4)],
        )

    def collect(self, value, mask):
        return self.mixed(
            value,
            [((2 * h + z // 2, z ^ mask), (2 * h + z // 2, z)) for h in (0, 1) for z in range(4)],
        )

    def ordered(self, flag, mine, other):
        first = jnp.where(flag == 0, mine, other)
        second = jnp.where(flag == 0, other, mine)
        return jnp.stack([first, second], 0)

    def over_shards(self, value):
        if self.n_shard == 2:
            return self.ordered(self.shard, value, self.shard_swap(value))
        return lax.all_gather(value, "shard", axis=0)

    def over_halves(self, value):
        return self.ordered(self.half, value, self.half_swap(value))

    def gather(self, piece):
        part, width = piece.shape
        both = self.ordered(self.core, piece, self.to_home(piece)).reshape(2 * part, width)
        near, far, cross = (self.spread(both, mask) for mask in (1, 2, 3))
        first = jnp.where(self.home, both, far)
        second = jnp.where(self.home, near, cross)
        first = self.over_halves(self.over_shards(first))
        first = jnp.moveaxis(first, 0, 1).reshape(-1, width)
        second = self.over_shards(self.over_halves(second)).reshape(-1, width)
        return first, second

    def reduce_halves(self, value, axis):
        sent = lax.dynamic_index_in_dim(value, 1 - self.half, axis, False).astype(LOW)
        kept = lax.dynamic_index_in_dim(value, self.half, axis, False)
        return kept + self.half_swap(sent).astype(SINGLE)

    def reduce_shards(self, value):
        if self.n_shard == 2:
            sent = lax.dynamic_index_in_dim(value, 1 - self.shard, 0, False).astype(LOW)
            kept = lax.dynamic_index_in_dim(value, self.shard, 0, False)
            return kept + self.shard_swap(sent).astype(SINGLE)
        return lax.psum_scatter(value, "shard", scatter_dimension=0, tiled=False)

    def scatter(self, first, second):
        rows, width = first.shape
        shape = (self.n_shard, 2, rows // (2 * self.n_shard), width)
        first = self.reduce_shards(self.reduce_halves(first.reshape(shape), 1))
        second = self.reduce_halves(self.reduce_shards(second.reshape(shape)), 0)
        low_first, low_second = first.astype(LOW), second.astype(LOW)
        near = self.collect(low_second, 1)
        far = self.mixed_far(low_first)
        cross = self.mixed_cross(low_second)
        total = first + near.astype(SINGLE) + far.astype(SINGLE) + cross.astype(SINGLE)
        pieces = total.reshape(2, -1, width)
        sent = lax.dynamic_index_in_dim(pieces, 1 - self.core, 0, False)
        kept = lax.dynamic_index_in_dim(pieces, self.core, 0, False)
        return jnp.where(self.home, kept, self.from_home(sent))

    def mixed_far(self, value):
        return self.collect(value, 2)

    def mixed_cross(self, value):
        return self.collect(value, 3)

    def over_tp(self, value):
        got = [value] + [self.tp_swap(value, mask) for mask in (1, 2, 3)]
        slots = []
        for slot in range(4):
            item = got[3]
            for mask in (0, 1, 2):
                item = jnp.where((self.tp ^ slot) == mask, got[mask], item)
            slots.append(item)
        return jnp.stack(slots, 0)

    def total(self, value):
        value = value + self.core_swap(value)
        value = value + self.half_swap(value)
        value = value + (
            self.shard_swap(value) if self.n_shard == 2 else lax.psum(value, "shard") - value
        )
        value = value + self.tp_swap(value, 1)
        return value + self.tp_swap(value, 2)


def columns(first, second, start, size):
    return jnp.concatenate([first[:, start : start + size], second[:, start : start + size]], 1)


def shards(
    tokens,
    lengths,
    first_gain,
    entry_weight,
    entry_bias,
    exit_weight,
    exit_bias,
    second_gain,
    hidden_weight,
    hidden_bias,
    return_weight,
    return_bias,
    cotangent,
):
    place = Place()
    local, narrow = tokens.shape[1:]
    part = entry_weight.shape[1]
    head_width = entry_weight.shape[2]
    units = hidden_weight.shape[1]

    entry_piece = jnp.moveaxis(entry_weight, 0, 1).reshape(part, 3 * head_width)
    rest_piece = jnp.concatenate([exit_weight.T, hidden_weight, return_weight.T], 1)
    entry_first, entry_second = place.gather(entry_piece)
    rest_first, rest_second = place.gather(rest_piece)
    weight_q = columns(entry_first, entry_second, 0, head_width)
    weight_kv = jnp.concatenate(
        [columns(entry_first, entry_second, at * head_width, head_width) for at in (1, 2)], 1
    )
    exit_t = columns(rest_first, rest_second, 0, head_width)
    hidden_full = columns(rest_first, rest_second, head_width, units)
    return_t = columns(rest_first, rest_second, head_width + units, units)
    biases = jnp.concatenate([entry_bias.reshape(-1), hidden_bias])
    bias_got = [biases] + [place.tp_swap(biases, mask) for mask in (1, 2, 3)]
    bias_first = jnp.where(place.home, bias_got[0], bias_got[2])
    bias_second = jnp.where(place.home, bias_got[1], bias_got[3])
    bias_two = jnp.stack([bias_first, bias_second])
    bias_q = bias_two[:, :head_width].reshape(-1)
    bias_v = bias_two[:, head_width : 2 * head_width].reshape(-1)
    bias_h = bias_two[:, 2 * head_width :].reshape(-1)

    length = lax.dynamic_index_in_dim(lengths, place.tp, 0, False)
    stream_part = lax.dynamic_index_in_dim(tokens, place.tp, 0, False).astype(SINGLE)
    stream = jnp.concatenate([stream_part, -jnp.sum(stream_part, -1, keepdims=True)], 1)
    first_inverse = lax.rsqrt(row_mean(stream * stream) + EPSILON)
    first_unit = stream * first_inverse
    normed_own = (first_unit * first_gain).astype(LOW)
    first_normed = jnp.concatenate([normed_own, place.core_swap(normed_own)], 0)

    position = place.ctx * local + jnp.arange(local, dtype=jnp.int32)
    valid = (position < length).astype(SINGLE)[:, None]
    cot_rows = lax.dynamic_index_in_dim(cotangent, place.tp, 0, False).astype(SINGLE) * valid
    cot_full = jnp.concatenate([cot_rows, jnp.zeros((local, 1), SINGLE)], 1)
    returned_grad_own = (cot_full - row_mean(cot_full)).astype(LOW)
    returned_grad = jnp.concatenate([returned_grad_own, place.core_swap(returned_grad_own)], 0)
    return_bias_grad = jnp.sum(returned_grad_own.astype(SINGLE), 0)

    bias_kv = jnp.concatenate([jnp.zeros_like(bias_v), bias_v])
    near_kv = (dot(first_normed, weight_kv) + bias_kv).astype(LOW)
    far_kv = place.half_up(near_kv)
    queries = (dot(first_normed, weight_q) + bias_q).astype(LOW)
    meta = jnp.stack([place.half, place.core, length]).astype(jnp.int32)
    attended, logs = attention_forward(meta, queries, near_kv, far_kv)

    def joined(partial):
        return partial[:local] + place.core_swap(partial[local:].astype(LOW)).astype(SINGLE)

    branch = joined(dot_nt(attended, exit_t)) + exit_bias
    middle = stream + branch - row_mean(branch)
    second_inverse = lax.rsqrt(row_mean(middle * middle) + EPSILON)
    second_unit = middle * second_inverse
    second_own = (second_unit * second_gain).astype(LOW)
    second_normed = jnp.concatenate([second_own, place.core_swap(second_own)], 0)
    hidden = dot(second_normed, hidden_full) + bias_h
    activated, gelu_pull = jax.vjp(
        lambda values_in: jax.nn.gelu(values_in, approximate=True), hidden
    )
    activated_low = activated.astype(LOW)
    hidden_grad = gelu_pull(dot(returned_grad, return_t))[0].astype(LOW)
    second_grad = joined(dot_nt(hidden_grad, hidden_full))
    returned = joined(dot_nt(activated_low, return_t)) + return_bias
    full_stream = middle + returned - row_mean(returned)
    result = place.over_tp(full_stream.astype(LOW))[:, :, :narrow]

    second_gain_grad = jnp.sum(second_grad * second_unit, 0)
    second_scaled = second_grad * second_gain
    middle_grad = cot_full + second_inverse * (
        second_scaled - second_unit * row_mean(second_scaled * second_unit)
    )
    branch_own = (middle_grad - row_mean(middle_grad)).astype(LOW)
    exit_bias_grad = jnp.sum(branch_own.astype(SINGLE), 0)
    branch_grad = jnp.concatenate([branch_own, place.core_swap(branch_own)], 0)
    attended_grad = dot(branch_grad, exit_t).astype(LOW)
    query_low, near_k, near_v, far_k, far_v = attention_backward(
        meta, queries, near_kv, far_kv, attended_grad, logs
    )
    back_kv = place.half_down(jnp.concatenate([far_k, far_v], 1))
    kv_low = (jnp.concatenate([near_k, near_v], 1) + back_kv.astype(SINGLE)).astype(LOW)
    first_grad = joined(dot_nt(query_low, weight_q) + dot_nt(kv_low, weight_kv))
    first_gain_grad = jnp.sum(first_grad * first_unit, 0)
    first_scaled = first_grad * first_gain
    stream_grad = middle_grad + first_inverse * (
        first_scaled - first_unit * row_mean(first_scaled * first_unit)
    )
    tokens_rows = (stream_grad - stream_grad[:, narrow:]).astype(LOW)
    tokens_grad = place.over_tp(tokens_rows)[:, :, :narrow]

    hidden_weight_grad = dot_tn(second_normed, hidden_grad)
    return_weight_grad = dot_tn(returned_grad, activated_low)
    mlp = place.scatter(
        *(
            jnp.concatenate(
                [hidden_weight_grad[:, cut], return_weight_grad[:, cut]], 1
            )
            for cut in (slice(0, units), slice(units, None))
        )
    )
    query_weight_grad = dot_tn(first_normed, query_low)
    kv_weight_grad = dot_tn(first_normed, kv_low)
    exit_weight_grad = dot_tn(branch_grad, attended)
    width = 2 * head_width
    heads = place.scatter(
        *(
            jnp.concatenate(
                [
                    query_weight_grad[:, at : at + head_width],
                    kv_weight_grad[:, at : at + head_width],
                    kv_weight_grad[:, width + at : width + at + head_width],
                    exit_weight_grad[:, at : at + head_width],
                ],
                1,
            )
            for at in (0, head_width)
        )
    )
    entry_grad = jnp.moveaxis(heads[:, : 3 * head_width].reshape(part, 3, head_width), 1, 0)
    exit_grad = heads[:, 3 * head_width :].T
    hidden_out = mlp[:, :units]
    return_out = mlp[:, units:].T

    query_sum = jnp.sum(query_low.astype(SINGLE), 0).reshape(2, head_width)
    value_sum = jnp.sum(kv_low[:, width:].astype(SINGLE), 0).reshape(2, head_width)
    hidden_sum = jnp.sum(hidden_grad.astype(SINGLE), 0).reshape(2, units)
    blocks = jnp.concatenate([query_sum, value_sum, hidden_sum], 1)
    first_id = jnp.where(place.home, place.tp, place.tp ^ 2)
    slots = []
    for slot in range(4):
        slots.append(
            jnp.where(first_id == slot, blocks[0], 0.0)
            + jnp.where(first_id == (slot ^ 1), blocks[1], 0.0)
        )
    vectors = jnp.concatenate(
        [first_gain_grad, exit_bias_grad, second_gain_grad, return_bias_grad] + slots
    )
    vectors = place.total(vectors)
    wide = narrow + 1
    mine = lax.dynamic_index_in_dim(vectors[4 * wide :].reshape(4, -1), place.tp, 0, False)
    return (
        result,
        tokens_grad,
        vectors[:wide],
        entry_grad,
        mine[:width].reshape(2, head_width),
        exit_grad,
        vectors[wide : 2 * wide],
        vectors[2 * wide : 3 * wide],
        hidden_out,
        mine[width:],
        return_out,
        vectors[3 * wide : 4 * wide],
    )


def solution(mesh):
    return jax.shard_map(
        shards,
        mesh=mesh,
        in_specs=(
            P("shard", "ctx", None),
            P("shard"),
            P(),
            P(None, ("shard", "ctx"), "tp"),
            P(None, "tp"),
            P("tp", ("shard", "ctx")),
            P(),
            P(),
            P(("shard", "ctx"), "tp"),
            P("tp"),
            P("tp", ("shard", "ctx")),
            P(),
            P("shard", "ctx", None),
        ),
        out_specs=(
            P("shard", "ctx", None),
            P("shard", "ctx", None),
            P(),
            P(None, ("shard", "ctx"), "tp"),
            P(None, "tp"),
            P("tp", ("shard", "ctx")),
            P(),
            P(),
            P(("shard", "ctx"), "tp"),
            P("tp"),
            P("tp", ("shard", "ctx")),
            P(),
        ),
        check_vma=False,
    )
```

```python
import functools
import math

import jax
import jax.numpy as jnp
from jax import lax
from jax.experimental import pallas as pl
from jax.experimental.pallas import tpu as pltpu
from jax.sharding import PartitionSpec as P

HDIM = 64
PAIR = 2 * HDIM
EPSILON = 1e-05
MASKED = -1e30
LOW = jnp.bfloat16
SINGLE = jnp.float32


def row_mean(values):
    return jnp.mean(values, -1, keepdims=True)


def dot(left, right):
    return jnp.dot(left, right, preferred_element_type=SINGLE)


def dot_nt(left, right):
    return lax.dot_general(left, right, (((1,), (1,)), ((), ())), preferred_element_type=SINGLE)


def dot_tn(left, right):
    return lax.dot_general(left, right, (((0,), (0,)), ((), ())), preferred_element_type=SINGLE)


def key_positions(meta, block, local, upper):
    base = upper * 2 * local + (meta[1] ^ block) * local
    return base + lax.broadcasted_iota(jnp.int32, (local, 1), 0)


def query_positions(meta, block, local):
    base = meta[0] * 2 * local + (meta[1] ^ block) * local
    return base + lax.broadcasted_iota(jnp.int32, (1, local), 1)


def masks(meta, block, local):
    near_pos = jnp.concatenate([key_positions(meta, b, local, meta[0]) for b in (0, 1)], 0)
    far_pos = jnp.concatenate([key_positions(meta, b, local, 0) for b in (0, 1)], 0)
    near = (near_pos <= query_positions(meta, block, local)) & (near_pos < meta[2])
    far = far_pos < jnp.where(meta[0] == 1, meta[2], 0)
    return near, far


def half_of(values, head):
    lanes = lax.broadcasted_iota(jnp.int32, values.shape, 1)
    return jnp.where((lanes >= HDIM) == (head == 1), values, jnp.zeros_like(values))


def forward_kernel(meta, q_ref, k_ref, v_ref, kf_ref, vf_ref, out_ref, log_ref):
    local = q_ref.shape[0] // 2
    scale = 1.0 / math.sqrt(HDIM)
    for block in (0, 1):
        near, far = masks(meta, block, local)
        rows = pl.ds(block * local, local)
        parts = []
        for head in (0, 1):
            query = half_of(q_ref[rows, :], head) * jnp.asarray(scale, LOW)
            near_s = jnp.where(near, dot_nt(k_ref[...], query), MASKED)
            far_s = jnp.where(far, dot_nt(kf_ref[...], query), MASKED)
            top = jnp.maximum(
                jnp.max(near_s, 0, keepdims=True), jnp.max(far_s, 0, keepdims=True)
            )
            near_p = jnp.exp(near_s - top)
            far_p = jnp.exp(far_s - top)
            total = jnp.sum(near_p, 0, keepdims=True) + jnp.sum(far_p, 0, keepdims=True)
            mixed = dot_tn(v_ref[...], near_p.astype(LOW)) + dot_tn(vf_ref[...], far_p.astype(LOW))
            parts.append(mixed[head * HDIM : (head + 1) * HDIM] / total)
            log_ref[0, head : head + 1, rows] = top + jnp.log(total)
        out_ref[rows, :] = jnp.concatenate(parts, 0).T.astype(LOW)


def attention_forward(meta, queries, near_kv, far_kv):
    rows, width = queries.shape
    pairs = width // PAIR
    block = functools.partial(pl.BlockSpec, (rows, PAIR))
    return pl.pallas_call(
        forward_kernel,
        grid_spec=pltpu.PrefetchScalarGridSpec(
            num_scalar_prefetch=1,
            grid=(pairs,),
            in_specs=[
                block(lambda j, meta: (0, j)),
                block(lambda j, meta: (0, j)),
                block(lambda j, meta: (0, pairs + j)),
                block(lambda j, meta: (0, j)),
                block(lambda j, meta: (0, pairs + j)),
            ],
            out_specs=[
                block(lambda j, meta: (0, j)),
                pl.BlockSpec((1, 2, rows), lambda j, meta: (j, 0, 0)),
            ],
        ),
        out_shape=[
            jax.ShapeDtypeStruct((rows, width), LOW),
            jax.ShapeDtypeStruct((pairs, 2, rows), SINGLE),
        ],
        cost_estimate=pl.CostEstimate(
            flops=8 * rows * rows * width * 2, bytes_accessed=rows * width * 14,
            transcendentals=2 * rows * rows * width // HDIM,
        ),
        name="attend",
    )(meta, queries, near_kv, near_kv, far_kv, far_kv)


def backward_kernel(
    meta, q_ref, k_ref, v_ref, kf_ref, vf_ref, grad_ref, log_ref,
    dq_ref, dk_ref, dv_ref, dkf_ref, dvf_ref, sums
):
    local = q_ref.shape[0] // 2
    scale = 1.0 / math.sqrt(HDIM)
    for block in (0, 1):
        near, far = masks(meta, block, local)
        rows = pl.ds(block * local, local)
        parts = []
        for head in (0, 1):
            query = half_of(q_ref[rows, :], head) * jnp.asarray(scale, LOW)
            out_grad = half_of(grad_ref[rows, :], head)
            log_total = log_ref[0, head : head + 1, rows]
            near_p = jnp.exp(jnp.where(near, dot_nt(k_ref[...], query), MASKED) - log_total)
            far_p = jnp.exp(jnp.where(far, dot_nt(kf_ref[...], query), MASKED) - log_total)
            near_g = dot_nt(v_ref[...], out_grad).astype(LOW).astype(SINGLE)
            far_g = dot_nt(vf_ref[...], out_grad).astype(LOW).astype(SINGLE)
            inner = jnp.sum(near_p * near_g, 0, keepdims=True) + jnp.sum(
                far_p * far_g, 0, keepdims=True
            )
            near_d = (near_p * (near_g - inner)).astype(LOW)
            far_d = (far_p * (far_g - inner)).astype(LOW)
            fresh = (
                dot(near_d, query), dot(near_p.astype(LOW), out_grad),
                dot(far_d, query), dot(far_p.astype(LOW), out_grad),
            )
            for at, value in enumerate(fresh):
                if block == 0 and head == 0:
                    sums[at] = value
                else:
                    sums[at] = sums[at] + value
            mixed = dot_tn(k_ref[...], near_d) + dot_tn(kf_ref[...], far_d)
            parts.append(mixed[head * HDIM : (head + 1) * HDIM] * scale)
        dq_ref[rows, :] = jnp.concatenate(parts, 0).T.astype(LOW)
    dk_ref[...] = sums[0]
    dv_ref[...] = sums[1]
    dkf_ref[...] = sums[2].astype(LOW)
    dvf_ref[...] = sums[3].astype(LOW)


def attention_backward(meta, queries, near_kv, far_kv, grads, logs):
    rows, width = queries.shape
    pairs = width // PAIR
    block = functools.partial(pl.BlockSpec, (rows, PAIR))
    same = lambda j, meta: (0, j)
    return pl.pallas_call(
        backward_kernel,
        grid_spec=pltpu.PrefetchScalarGridSpec(
            num_scalar_prefetch=1,
            grid=(pairs,),
            in_specs=[
                block(same),
                block(same),
                block(lambda j, meta: (0, pairs + j)),
                block(same),
                block(lambda j, meta: (0, pairs + j)),
                block(same),
                pl.BlockSpec((1, 2, rows), lambda j, meta: (j, 0, 0)),
            ],
            out_specs=[block(same)] * 5,
            scratch_shapes=[pltpu.VMEM((4, rows, PAIR), SINGLE)],
        ),
        out_shape=[
            jax.ShapeDtypeStruct((rows, width), LOW),
            jax.ShapeDtypeStruct((rows, width), SINGLE),
            jax.ShapeDtypeStruct((rows, width), SINGLE),
            jax.ShapeDtypeStruct((rows, width), LOW),
            jax.ShapeDtypeStruct((rows, width), LOW),
        ],
        cost_estimate=pl.CostEstimate(
            flops=20 * rows * rows * width * 2, bytes_accessed=rows * width * 30,
            transcendentals=2 * rows * rows * width // HDIM,
        ),
        name="attend_back",
    )(meta, queries, near_kv, near_kv, far_kv, far_kv, grads, logs)


def after(value, *gates):
    return lax.optimization_barrier((value, *gates))[0]


class Place:
    def __init__(self):
        self.n_shard = lax.axis_size("shard")
        self.n_ctx = lax.axis_size("ctx")
        self.n_tp = lax.axis_size("tp")
        self.shard = lax.axis_index("shard")
        self.ctx = lax.axis_index("ctx")
        self.half = self.ctx // 2
        self.core = self.ctx % 2
        self.tp = lax.axis_index("tp")
        self.home = self.core == self.tp // 2

    def core_swap(self, value):
        return lax.ppermute(value, "ctx", [(i, i ^ 1) for i in range(self.n_ctx)])

    def half_swap(self, value):
        return lax.ppermute(value, "ctx", [(i, i ^ 2) for i in range(self.n_ctx)])

    def half_up(self, value):
        return lax.ppermute(value, "ctx", [(0, 2), (1, 3)])

    def half_down(self, value):
        return lax.ppermute(value, "ctx", [(2, 0), (3, 1)])

    def shard_swap(self, value):
        return lax.ppermute(value, "shard", [(0, 1), (1, 0)])

    def tp_swap(self, value, mask):
        return lax.ppermute(value, "tp", [(i, i ^ mask) for i in range(self.n_tp)])

    def ordered(self, flag, mine, other, axis=0):
        first = jnp.where(flag == 0, mine, other)
        second = jnp.where(flag == 0, other, mine)
        return jnp.stack([first, second], axis)


    def own_block(self, piece, far):
        kept = jnp.where(self.home, piece, far)
        sent = jnp.where(self.home, far, piece)
        return self.ordered(self.core, kept, self.core_swap(sent)).reshape(-1, piece.shape[1])

    def over_shards(self, value):
        if self.n_shard == 2:
            return self.ordered(self.shard, value, self.shard_swap(value))
        return lax.all_gather(value, "shard", axis=0)

    def rows_half_first(self, block):
        value = self.over_shards(self.ordered(self.half, block, self.half_swap(block)))
        return value.reshape(-1, block.shape[1])

    def rows_shard_first(self, block):
        value = self.over_shards(block)
        value = self.ordered(self.half, value, self.half_swap(value), 1)
        return value.reshape(-1, block.shape[1])


    def split_rows(self, value):
        rows, width = value.shape
        return value.reshape(self.n_shard, 2, rows // (2 * self.n_shard), width)

    def half_step(self, value, axis):
        sent = lax.dynamic_index_in_dim(value, 1 - self.half, axis, False).astype(LOW)
        kept = lax.dynamic_index_in_dim(value, self.half, axis, False)
        return kept, self.half_swap(sent)

    def shard_step(self, value):
        if self.n_shard == 2:
            sent = lax.dynamic_index_in_dim(value, 1 - self.shard, 0, False).astype(LOW)
            kept = lax.dynamic_index_in_dim(value, self.shard, 0, False)
            return kept, self.shard_swap(sent)
        kept = lax.psum_scatter(value, "shard", scatter_dimension=0, tiled=False)
        return kept, jnp.zeros_like(kept, LOW)

    def block_step(self, value):
        pieces = value.reshape(2, -1, value.shape[1])
        sent = lax.dynamic_index_in_dim(pieces, 1 - self.core, 0, False).astype(LOW)
        kept = lax.dynamic_index_in_dim(pieces, self.core, 0, False)
        got = self.core_swap(sent).astype(SINGLE)
        sent = jnp.where(self.home, got, kept).astype(LOW)
        return jnp.where(self.home, kept, got), self.tp_swap(sent, 2)

    def tp_far(self, value):
        return self.ordered(self.tp // 2, value, self.tp_swap(value, 2))

    def tp_all(self, pair):
        value = self.ordered(self.tp % 2, pair, self.tp_swap(pair, 1), 1)
        return value.reshape(4, *pair.shape[1:])

    def total(self, value):
        value = value + self.core_swap(value)
        value = value + self.half_swap(value)
        value = value + (
            self.shard_swap(value) if self.n_shard == 2 else lax.psum(value, "shard") - value
        )
        value = value + self.tp_swap(value, 1)
        return value + self.tp_swap(value, 2)


def added(step, *gates):
    kept, arriving = step
    return kept + after(arriving, *gates).astype(SINGLE)


def interleaved(first, second, width):
    parts = []
    for start in range(0, first.shape[1], width):
        parts += [first[:, start : start + width], second[:, start : start + width]]
    return jnp.concatenate(parts, 1)


def shards(
    tokens,
    lengths,
    first_gain,
    entry_weight,
    entry_bias,
    exit_weight,
    exit_bias,
    second_gain,
    hidden_weight,
    hidden_bias,
    return_weight,
    return_bias,
    cotangent,
):
    place = Place()
    local, narrow = tokens.shape[1:]
    part = entry_weight.shape[1]
    head_width = entry_weight.shape[2]
    units = hidden_weight.shape[1]

    width = 2 * head_width

    piece_a = jnp.concatenate([entry_weight[1], entry_weight[2], entry_weight[0], exit_weight.T], 1)
    piece_b = jnp.concatenate([hidden_weight, return_weight.T], 1)
    biases = jnp.concatenate([entry_bias.reshape(-1), hidden_bias])
    far_a = place.tp_swap(piece_a, 2)
    bias_mine = jnp.where(place.home, biases, place.tp_swap(biases, 2))
    bias_two = jnp.stack([bias_mine, place.tp_swap(bias_mine, 1)])
    bias_q = bias_two[:, :head_width].reshape(-1)
    bias_v = bias_two[:, head_width:width].reshape(-1)
    bias_h = bias_two[:, width:].reshape(-1)
    mine_a = place.own_block(piece_a, far_a)
    other_a = place.tp_swap(mine_a, 1)
    block_kv = interleaved(mine_a[:, :width], other_a[:, :width], head_width)
    block_qe = interleaved(mine_a[:, width:], other_a[:, width:], head_width)
    weight_kv = place.rows_half_first(block_kv)
    weight_qe = place.rows_shard_first(block_qe)
    weight_q, exit_t = weight_qe[:, :width], weight_qe[:, width:]
    piece_b = after(piece_b, other_a)
    mine_b = place.own_block(piece_b, place.tp_swap(piece_b, 2))
    other_b = place.tp_swap(mine_b, 1)

    length = lax.dynamic_index_in_dim(lengths, place.tp, 0, False)
    tokens_low, cot_low = (
        lax.dynamic_index_in_dim(item, place.tp, 0, False) for item in (tokens, cotangent)
    )
    stream_part = after(tokens_low, far_a).astype(SINGLE)
    stream = jnp.concatenate([stream_part, -jnp.sum(stream_part, -1, keepdims=True)], 1)
    first_inverse = lax.rsqrt(row_mean(stream * stream) + EPSILON)
    first_unit = stream * first_inverse
    normed_own = (first_unit * first_gain).astype(LOW)
    position = place.ctx * local + jnp.arange(local, dtype=jnp.int32)
    valid = (position < length).astype(SINGLE)[:, None]
    cot_rows = cot_low.astype(SINGLE) * valid
    cot_full = jnp.concatenate([cot_rows, jnp.zeros((local, 1), SINGLE)], 1)
    returned_own = (cot_full - row_mean(cot_full)).astype(LOW)
    own_two = jnp.concatenate([normed_own, returned_own], 1)
    all_two = jnp.concatenate([own_two, place.core_swap(own_two)], 0)
    wide = narrow + 1
    first_normed, returned_grad = all_two[:, :wide], all_two[:, wide:]

    bias_kv = jnp.concatenate([jnp.zeros_like(bias_v), bias_v])
    near_kv = (dot(first_normed, weight_kv) + bias_kv).astype(LOW)
    far_kv = place.half_up(near_kv)
    block_h = jnp.concatenate([mine_b[:, :units], other_b[:, :units]], 1)
    block_r = jnp.concatenate([mine_b[:, units:], other_b[:, units:]], 1)
    block_h, block_r = after((block_h, block_r), near_kv, weight_qe)
    hidden_full = place.rows_half_first(block_h)
    return_t = place.rows_shard_first(block_r)
    queries = (dot(first_normed, weight_q) + bias_q).astype(LOW)
    meta = jnp.stack([place.half, place.core, length]).astype(jnp.int32)
    attended, logs = attention_forward(meta, queries, near_kv, far_kv)

    def joined(partial, *gates):
        return added((partial[:local], place.core_swap(partial[local:].astype(LOW))), *gates)

    branch = joined(dot_nt(attended, exit_t)) + exit_bias
    middle = stream + branch - row_mean(branch)
    second_inverse = lax.rsqrt(row_mean(middle * middle) + EPSILON)
    second_unit = middle * second_inverse
    second_own = (second_unit * second_gain).astype(LOW)
    second_normed = jnp.concatenate([second_own, place.core_swap(second_own)], 0)
    hidden = dot(second_normed, hidden_full) + bias_h
    activated, gelu_pull = jax.vjp(
        lambda values_in: jax.nn.gelu(values_in, approximate=True), hidden
    )
    activated_low = activated.astype(LOW)
    hidden_grad = gelu_pull(dot(returned_grad, return_t))[0].astype(LOW)
    second_part = dot_nt(hidden_grad, hidden_full)
    returned_part = dot_nt(activated_low, return_t)
    second_grad = joined(second_part)
    returned = joined(returned_part, second_part) + return_bias
    full_stream = middle + returned - row_mean(returned)
    result_own = full_stream.astype(LOW)

    hidden_weight_grad = dot_tn(second_normed, hidden_grad)
    return_weight_grad = dot_tn(returned_grad, after(activated_low, second_part))
    step_h = place.half_step(place.split_rows(hidden_weight_grad), 1)
    step_r = place.shard_step(place.split_rows(return_weight_grad))

    second_gain_grad = jnp.sum(second_grad * second_unit, 0)
    second_scaled = second_grad * second_gain
    middle_grad = cot_full + second_inverse * (
        second_scaled - second_unit * row_mean(second_scaled * second_unit)
    )
    branch_own = (middle_grad - row_mean(middle_grad)).astype(LOW)
    branch_grad = jnp.concatenate([branch_own, place.core_swap(branch_own)], 0)
    result_far = place.tp_far(result_own)
    attended_grad = dot(branch_grad, exit_t).astype(LOW)
    query_low, near_k, near_v, far_k, far_v = attention_backward(
        meta, queries, near_kv, far_kv, attended_grad, logs
    )
    back_kv = place.half_down(jnp.concatenate([far_k, far_v], 1))
    result_all = place.tp_all(after(result_far, query_low))
    step_h = place.shard_step(added(step_h, query_low))
    step_r = place.half_step(added(step_r, query_low), 0)
    query_weight_grad = dot_tn(first_normed, query_low)
    exit_weight_grad = dot_tn(branch_grad, attended)
    query_part = dot_nt(query_low, weight_q)
    kv_low = (
        jnp.concatenate([near_k, near_v], 1)
        + after(back_kv, query_weight_grad, exit_weight_grad, query_part).astype(SINGLE)
    ).astype(LOW)
    first_part = query_part + dot_nt(kv_low, weight_kv)
    first_grad = joined(first_part)
    first_scaled = first_grad * first_gain
    stream_grad = middle_grad + first_inverse * (
        first_scaled - first_unit * row_mean(first_scaled * first_unit)
    )
    tokens_rows = (stream_grad - stream_grad[:, narrow:]).astype(LOW)
    tokens_far = place.tp_far(tokens_rows)

    sum_h, sum_r = added(step_h, first_part), added(step_r, first_part)
    mlp = (
        jnp.concatenate([sum_h[:, :units], sum_r[:, :units]], 1),
        place.tp_swap(
            jnp.concatenate([sum_h[:, units:], sum_r[:, units:]], 1).astype(LOW), 1
        ),
    )
    kv_weight_grad = dot_tn(first_normed, kv_low)
    step_kv = place.half_step(place.split_rows(kv_weight_grad), 1)
    step_qe = place.shard_step(
        place.split_rows(jnp.concatenate([query_weight_grad, exit_weight_grad], 1))
    )
    mlp = place.block_step(added(mlp, tokens_rows))
    step_kv = place.shard_step(added(step_kv, tokens_rows))
    step_qe = place.half_step(added(step_qe, tokens_rows), 0)
    tokens_all = place.tp_all(tokens_far)
    sums = jnp.concatenate([added(step_qe), added(step_kv)], 1)
    sums = [
        jnp.concatenate([sums[:, at * width + low : at * width + low + head_width] for at in range(4)], 1)
        for low in (0, head_width)
    ]
    heads = place.block_step(added((sums[0], place.tp_swap(sums[1].astype(LOW), 1))))
    mlp = added(mlp, tokens_all)
    heads = added(heads, tokens_all)
    result = after(result_all, tokens_rows)[:, :, :narrow]
    tokens_grad = tokens_all[:, :, :narrow]
    at = lambda index: heads[:, index * head_width : (index + 1) * head_width]
    entry_grad = jnp.stack([at(0), at(2), at(3)])
    exit_grad = at(1).T
    hidden_out = mlp[:, :units]
    return_out = mlp[:, units:].T

    return_bias_grad = jnp.sum(returned_own.astype(SINGLE), 0)
    exit_bias_grad = jnp.sum(branch_own.astype(SINGLE), 0)
    first_gain_grad = jnp.sum(first_grad * first_unit, 0)
    query_sum = jnp.sum(query_low.astype(SINGLE), 0).reshape(2, head_width)
    value_sum = jnp.sum(kv_low[:, width:].astype(SINGLE), 0).reshape(2, head_width)
    hidden_sum = jnp.sum(hidden_grad.astype(SINGLE), 0).reshape(2, units)
    blocks = jnp.concatenate([query_sum, value_sum, hidden_sum], 1)
    first_id = jnp.where(place.home, place.tp, place.tp ^ 2)
    slots = []
    for slot in range(4):
        slots.append(
            jnp.where(first_id == slot, blocks[0], 0.0)
            + jnp.where(first_id == (slot ^ 1), blocks[1], 0.0)
        )
    vectors = jnp.concatenate(
        [first_gain_grad, exit_bias_grad, second_gain_grad, return_bias_grad] + slots
    )
    vectors = place.total(vectors)
    own = lax.dynamic_index_in_dim(vectors[4 * wide :].reshape(4, -1), place.tp, 0, False)
    return (
        result,
        tokens_grad,
        vectors[:wide],
        entry_grad,
        own[:width].reshape(2, head_width),
        exit_grad,
        vectors[wide : 2 * wide],
        vectors[2 * wide : 3 * wide],
        hidden_out,
        own[width:],
        return_out,
        vectors[3 * wide : 4 * wide],
    )


def solution(mesh):
    return jax.shard_map(
        shards,
        mesh=mesh,
        in_specs=(
            P("shard", "ctx", None),
            P("shard"),
            P(),
            P(None, ("shard", "ctx"), "tp"),
            P(None, "tp"),
            P("tp", ("shard", "ctx")),
            P(),
            P(),
            P(("shard", "ctx"), "tp"),
            P("tp"),
            P("tp", ("shard", "ctx")),
            P(),
            P("shard", "ctx", None),
        ),
        out_specs=(
            P("shard", "ctx", None),
            P("shard", "ctx", None),
            P(),
            P(None, ("shard", "ctx"), "tp"),
            P(None, "tp"),
            P("tp", ("shard", "ctx")),
            P(),
            P(),
            P(("shard", "ctx"), "tp"),
            P("tp"),
            P("tp", ("shard", "ctx")),
            P(),
        ),
        check_vma=False,
    )
```

```python
import functools
import math

import jax
import jax.numpy as jnp
from jax import lax
from jax.experimental import pallas as pl
from jax.experimental.pallas import tpu as pltpu
from jax.sharding import PartitionSpec as P

HDIM = 64
PAIR = 2 * HDIM
EPSILON = 1e-05
MASKED = -1e30
LOW = jnp.bfloat16
SINGLE = jnp.float32


def row_mean(values):
    return jnp.mean(values, -1, keepdims=True)


def dot(left, right):
    return jnp.dot(left, right, preferred_element_type=SINGLE)


def dot_nt(left, right):
    return lax.dot_general(left, right, (((1,), (1,)), ((), ())), preferred_element_type=SINGLE)


def dot_tn(left, right):
    return lax.dot_general(left, right, (((0,), (0,)), ((), ())), preferred_element_type=SINGLE)


def key_positions(meta, block, local, upper):
    base = upper * 2 * local + (meta[1] ^ block) * local
    return base + lax.broadcasted_iota(jnp.int32, (local, 1), 0)


def query_positions(meta, block, local):
    base = meta[0] * 2 * local + (meta[1] ^ block) * local
    return base + lax.broadcasted_iota(jnp.int32, (1, local), 1)


def near_mask(meta, block, local):
    position = jnp.concatenate([key_positions(meta, b, local, meta[0]) for b in (0, 1)], 0)
    return (position <= query_positions(meta, block, local)) & (position < meta[2])


def far_mask(meta, local):
    position = jnp.concatenate([key_positions(meta, b, local, 0) for b in (0, 1)], 0)
    return position < jnp.where(meta[0] == 1, meta[2], 0)


def half_of(values, head):
    lanes = lax.broadcasted_iota(jnp.int32, values.shape, 1)
    return jnp.where((lanes >= HDIM) == (head == 1), values, jnp.zeros_like(values))


def head_rows(head):
    return slice(head * HDIM, (head + 1) * HDIM)


def forward_kernel(meta, q_ref, k_ref, v_ref, kf_ref, vf_ref, out_ref, log_ref):
    local = q_ref.shape[0] // 2
    scale = jnp.asarray(1.0 / math.sqrt(HDIM), LOW)
    far = far_mask(meta, local)
    for block in (0, 1):
        near = near_mask(meta, block, local)
        rows = pl.ds(block * local, local)
        parts = []
        for head in (0, 1):
            query = half_of(q_ref[rows, :], head) * scale
            near_s = jnp.where(near, dot_nt(k_ref[...], query), MASKED)
            far_s = jnp.where(far, dot_nt(kf_ref[...], query), MASKED)
            top = jnp.maximum(
                jnp.max(near_s, 0, keepdims=True), jnp.max(far_s, 0, keepdims=True)
            )
            near_p = jnp.exp(near_s - top)
            far_p = jnp.exp(far_s - top)
            total = jnp.sum(near_p, 0, keepdims=True) + jnp.sum(far_p, 0, keepdims=True)
            mixed = dot_tn(v_ref[...], near_p.astype(LOW)) + dot_tn(vf_ref[...], far_p.astype(LOW))
            parts.append(mixed[head_rows(head)] / total)
            log_ref[0, head : head + 1, rows] = top + jnp.log(total)
        out_ref[rows, :] = jnp.concatenate(parts, 0).T.astype(LOW)


def far_backward_kernel(
    meta, q_ref, k_ref, v_ref, grad_ref, out_ref, log_ref, dkv_ref, inner_ref, mix_ref, sums
):
    rows_all, width = q_ref.shape[0], dkv_ref.shape[1] // 2
    local = rows_all // 2
    scale = jnp.asarray(1.0 / math.sqrt(HDIM), LOW)
    mask = far_mask(meta, local)
    for block in (0, 1):
        rows = pl.ds(block * local, local)
        product = (grad_ref[rows, :].astype(SINGLE) * out_ref[rows, :].astype(SINGLE)).T
        for head in (0, 1):
            query = half_of(q_ref[rows, :], head) * scale
            out_grad = half_of(grad_ref[rows, :], head)
            log_total = log_ref[0, head : head + 1, rows]
            inner = jnp.sum(product[head_rows(head)], 0, keepdims=True)
            inner_ref[0, head : head + 1, rows] = inner
            probs = jnp.exp(jnp.where(mask, dot_nt(k_ref[...], query), MASKED) - log_total)
            grads = (probs * (dot_nt(v_ref[...], out_grad) - inner)).astype(LOW)
            fresh = dot(grads, query), dot(probs.astype(LOW), out_grad)
            for at, value in enumerate(fresh):
                sums[at] = value if block == 0 and head == 0 else sums[at] + value
            mix_ref[0, head_rows(head), rows] = dot_tn(k_ref[...], grads)[head_rows(head)]
    lanes = pl.multiple_of(pl.program_id(0) * PAIR, PAIR)
    dkv_ref[:, pl.ds(lanes, PAIR)] = sums[0].astype(LOW)
    dkv_ref[:, pl.ds(width + lanes, PAIR)] = sums[1].astype(LOW)


def near_backward_kernel(
    meta, q_ref, k_ref, v_ref, grad_ref, log_ref, inner_ref, mix_ref, dq_ref, dkv_ref, sums
):
    rows_all, width = q_ref.shape[0], dkv_ref.shape[1] // 2
    local = rows_all // 2
    scale = 1.0 / math.sqrt(HDIM)
    for block in (0, 1):
        mask = near_mask(meta, block, local)
        rows = pl.ds(block * local, local)
        parts = []
        for head in (0, 1):
            query = half_of(q_ref[rows, :], head) * jnp.asarray(scale, LOW)
            out_grad = half_of(grad_ref[rows, :], head)
            log_total = log_ref[0, head : head + 1, rows]
            inner = inner_ref[0, head : head + 1, rows]
            probs = jnp.exp(jnp.where(mask, dot_nt(k_ref[...], query), MASKED) - log_total)
            grads = (probs * (dot_nt(v_ref[...], out_grad) - inner)).astype(LOW)
            fresh = dot(grads, query), dot(probs.astype(LOW), out_grad)
            for at, value in enumerate(fresh):
                sums[at] = value if block == 0 and head == 0 else sums[at] + value
            mixed = dot_tn(k_ref[...], grads)[head_rows(head)]
            parts.append((mix_ref[0, head_rows(head), rows] + mixed) * scale)
        dq_ref[rows, :] = jnp.concatenate(parts, 0).T.astype(LOW)
    lanes = pl.multiple_of(pl.program_id(0) * PAIR, PAIR)
    dkv_ref[:, pl.ds(lanes, PAIR)] = sums[0].astype(LOW)
    dkv_ref[:, pl.ds(width + lanes, PAIR)] = sums[1].astype(LOW)


def attention_call(kernel, name, meta, rows, width, operands, outs, scratch=()):
    pairs = width // PAIR
    specs = {
        "pair": ((rows, PAIR), lambda j, meta: (0, j), (rows, width)),
        "value": ((rows, PAIR), lambda j, meta: (0, pairs + j), None),
        "row": ((1, 2, rows), lambda j, meta: (j, 0, 0), (pairs, 2, rows)),
        "mix": ((1, PAIR, rows), lambda j, meta: (j, 0, 0), (pairs, PAIR, rows)),
        "all": ((rows, 2 * width), lambda j, meta: (0, 0), (rows, 2 * width)),
    }
    return pl.pallas_call(
        kernel,
        grid_spec=pltpu.PrefetchScalarGridSpec(
            num_scalar_prefetch=1,
            grid=(pairs,),
            in_specs=[pl.BlockSpec(*specs[kind][:2]) for kind, _ in operands],
            out_specs=[pl.BlockSpec(*specs[kind][:2]) for kind, _ in outs],
            scratch_shapes=list(scratch),
        ),
        out_shape=[jax.ShapeDtypeStruct(specs[kind][2], dtype) for kind, dtype in outs],
        cost_estimate=pl.CostEstimate(
            flops=8 * rows * rows * width, bytes_accessed=rows * width * 16,
            transcendentals=rows * rows * width // HDIM,
        ),
        name=name,
    )(meta, *(array for _, array in operands))


def attend(meta, queries, near_kv, far_kv):
    return attention_call(
        forward_kernel, "attend", meta, *queries.shape,
        [("pair", queries), ("pair", near_kv), ("value", near_kv), ("pair", far_kv),
         ("value", far_kv)],
        [("pair", LOW), ("row", SINGLE)],
    )


def attend_far_back(meta, queries, kv, grads, attended, logs):
    rows, width = queries.shape
    return attention_call(
        far_backward_kernel, "attend_far_back", meta, rows, width,
        [("pair", queries), ("pair", kv), ("value", kv), ("pair", grads), ("pair", attended),
         ("row", logs)],
        [("all", LOW), ("row", SINGLE), ("mix", SINGLE)],
        [pltpu.VMEM((2, rows, PAIR), SINGLE)],
    )


def attend_near_back(meta, queries, kv, grads, logs, inner, mixed):
    rows, width = queries.shape
    return attention_call(
        near_backward_kernel, "attend_near_back", meta, rows, width,
        [("pair", queries), ("pair", kv), ("value", kv), ("pair", grads), ("row", logs),
         ("row", inner), ("mix", mixed)],
        [("pair", LOW), ("all", LOW)],
        [pltpu.VMEM((2, rows, PAIR), SINGLE)],
    )


def after(value, *gates):
    return lax.optimization_barrier((value, *gates))[0]


class Place:
    def __init__(self):
        self.n_shard = lax.axis_size("shard")
        self.n_ctx = lax.axis_size("ctx")
        self.n_tp = lax.axis_size("tp")
        self.shard = lax.axis_index("shard")
        self.ctx = lax.axis_index("ctx")
        self.half = self.ctx // 2
        self.core = self.ctx % 2
        self.tp = lax.axis_index("tp")
        self.home = self.core == self.tp // 2

    def core_swap(self, value):
        return lax.ppermute(value, "ctx", [(i, i ^ 1) for i in range(self.n_ctx)])

    def half_swap(self, value):
        return lax.ppermute(value, "ctx", [(i, i ^ 2) for i in range(self.n_ctx)])

    def half_up(self, value):
        return lax.ppermute(value, "ctx", [(0, 2), (1, 3)])

    def half_down(self, value):
        return lax.ppermute(value, "ctx", [(2, 0), (3, 1)])

    def shard_swap(self, value):
        return lax.ppermute(value, "shard", [(0, 1), (1, 0)])

    def tp_swap(self, value, mask):
        return lax.ppermute(value, "tp", [(i, i ^ mask) for i in range(self.n_tp)])

    def ordered(self, flag, mine, other, axis=0):
        first = jnp.where(flag == 0, mine, other)
        second = jnp.where(flag == 0, other, mine)
        return jnp.stack([first, second], axis)


    def own_block(self, piece, far):
        kept = jnp.where(self.home, piece, far)
        sent = jnp.where(self.home, far, piece)
        return self.ordered(self.core, kept, self.core_swap(sent)).reshape(-1, piece.shape[1])

    def over_shards(self, value):
        if self.n_shard == 2:
            return self.ordered(self.shard, value, self.shard_swap(value))
        return lax.all_gather(value, "shard", axis=0)

    def rows_half_first(self, block):
        value = self.over_shards(self.ordered(self.half, block, self.half_swap(block)))
        return value.reshape(-1, block.shape[1])

    def rows_shard_first(self, block):
        value = self.over_shards(block)
        value = self.ordered(self.half, value, self.half_swap(value), 1)
        return value.reshape(-1, block.shape[1])


    def split_rows(self, value):
        rows, width = value.shape
        return value.reshape(self.n_shard, 2, rows // (2 * self.n_shard), width)

    def half_step(self, value, axis):
        sent = lax.dynamic_index_in_dim(value, 1 - self.half, axis, False).astype(LOW)
        kept = lax.dynamic_index_in_dim(value, self.half, axis, False)
        return kept, self.half_swap(sent)

    def shard_step(self, value):
        if self.n_shard == 2:
            sent = lax.dynamic_index_in_dim(value, 1 - self.shard, 0, False).astype(LOW)
            kept = lax.dynamic_index_in_dim(value, self.shard, 0, False)
            return kept, self.shard_swap(sent)
        kept = lax.psum_scatter(value, "shard", scatter_dimension=0, tiled=False)
        return kept, jnp.zeros_like(kept, LOW)

    def block_step(self, value):
        pieces = value.reshape(2, -1, value.shape[1])
        sent = lax.dynamic_index_in_dim(pieces, 1 - self.core, 0, False).astype(LOW)
        kept = lax.dynamic_index_in_dim(pieces, self.core, 0, False)
        got = self.core_swap(sent).astype(SINGLE)
        sent = jnp.where(self.home, got, kept).astype(LOW)
        return jnp.where(self.home, kept, got), self.tp_swap(sent, 2)

    def tp_all(self, pair, arriving):
        value = self.ordered(self.tp % 2, pair, arriving, 1)
        return value.reshape(4, *pair.shape[1:])

    def chip_total(self, value):
        value = value + self.core_swap(value)
        value = value + self.half_swap(value)
        if self.n_shard == 2:
            return value + self.shard_swap(value)
        return lax.psum(value, "shard")

    def tp_total(self, value):
        value = value + self.tp_swap(value, 1)
        return value + self.tp_swap(value, 2)


def added(step, *gates):
    kept, arriving = step
    return kept + after(arriving, *gates).astype(SINGLE)


def interleaved(first, second, width):
    parts = []
    for start in range(0, first.shape[1], width):
        parts += [first[:, start : start + width], second[:, start : start + width]]
    return jnp.concatenate(parts, 1)


def shards(
    tokens,
    lengths,
    first_gain,
    entry_weight,
    entry_bias,
    exit_weight,
    exit_bias,
    second_gain,
    hidden_weight,
    hidden_bias,
    return_weight,
    return_bias,
    cotangent,
):
    place = Place()
    local, narrow = tokens.shape[1:]
    part = entry_weight.shape[1]
    head_width = entry_weight.shape[2]
    units = hidden_weight.shape[1]

    width = 2 * head_width

    piece_a = jnp.concatenate([entry_weight[1], entry_weight[2], entry_weight[0], exit_weight.T], 1)
    piece_b = jnp.concatenate([hidden_weight, return_weight.T], 1)
    biases = jnp.concatenate([entry_bias.reshape(-1), hidden_bias])
    far_a = place.tp_swap(piece_a, 2)
    bias_mine = jnp.where(place.home, biases, place.tp_swap(biases, 2))
    bias_two = jnp.stack([bias_mine, place.tp_swap(bias_mine, 1)])
    bias_q = bias_two[:, :head_width].reshape(-1)
    bias_v = bias_two[:, head_width:width].reshape(-1)
    bias_h = bias_two[:, width:].reshape(-1)
    mine_a = place.own_block(piece_a, far_a)
    other_a = place.tp_swap(mine_a, 1)

    length = lax.dynamic_index_in_dim(lengths, place.tp, 0, False)
    tokens_low, cot_low = (
        lax.dynamic_index_in_dim(item, place.tp, 0, False) for item in (tokens, cotangent)
    )
    stream_part = after(tokens_low, far_a).astype(SINGLE)
    stream = jnp.concatenate([stream_part, -jnp.sum(stream_part, -1, keepdims=True)], 1)
    first_inverse = lax.rsqrt(row_mean(stream * stream) + EPSILON)
    first_unit = stream * first_inverse
    normed_own = (first_unit * first_gain).astype(LOW)
    far_own = place.half_up(normed_own)
    position = place.ctx * local + jnp.arange(local, dtype=jnp.int32)
    valid = (position < length).astype(SINGLE)[:, None]
    cot_rows = cot_low.astype(SINGLE) * valid
    cot_full = jnp.concatenate([cot_rows, jnp.zeros((local, 1), SINGLE)], 1)
    returned_own = (cot_full - row_mean(cot_full)).astype(LOW)
    own_two = jnp.concatenate([normed_own, returned_own], 1)
    all_two = jnp.concatenate([own_two, place.core_swap(own_two)], 0)
    wide = narrow + 1
    first_normed, returned_grad = all_two[:, :wide], all_two[:, wide:]

    block_kv = interleaved(mine_a[:, :width], other_a[:, :width], head_width)
    block_qe = interleaved(mine_a[:, width:], other_a[:, width:], head_width)
    half_kv = place.ordered(place.half, block_kv, place.half_swap(block_kv))
    weight_kv = place.over_shards(half_kv).reshape(-1, 2 * width)
    weight_qe = place.rows_shard_first(block_qe)
    weight_q, exit_t = weight_qe[:, :width], weight_qe[:, width:]
    piece_b = after(piece_b, other_a)
    mine_b = place.own_block(piece_b, place.tp_swap(piece_b, 2))
    other_b = place.tp_swap(mine_b, 1)

    far_own = after(far_own, half_kv)
    far_normed = jnp.concatenate([far_own, place.core_swap(far_own)], 0)
    bias_kv = jnp.concatenate([jnp.zeros_like(bias_v), bias_v])
    block_h = jnp.concatenate([mine_b[:, :units], other_b[:, :units]], 1)
    block_r = jnp.concatenate([mine_b[:, units:], other_b[:, units:]], 1)
    block_h, block_r = after((block_h, block_r), weight_kv, weight_qe)
    half_h = place.ordered(place.half, block_h, place.half_swap(block_h))
    shard_r = place.over_shards(block_r)
    hidden_full = place.over_shards(half_h).reshape(-1, 2 * units)
    return_t = place.ordered(place.half, shard_r, place.half_swap(shard_r), 1)
    return_t = return_t.reshape(-1, 2 * units)
    near_kv = (dot(first_normed, weight_kv) + bias_kv).astype(LOW)
    far_kv = (dot(far_normed, weight_kv) + bias_kv).astype(LOW)
    queries = (dot(first_normed, after(weight_q, block_h, block_r)) + bias_q).astype(LOW)
    meta = jnp.stack([place.half, place.core, length]).astype(jnp.int32)
    attended, logs = attend(meta, queries, near_kv, after(far_kv, half_h, shard_r))

    def joined(product, left, weight):
        sent = product(left[local:], weight).astype(LOW)
        return product(after(left[:local], sent), weight), place.core_swap(sent)

    branch = added(joined(dot_nt, attended, exit_t)) + exit_bias
    middle = stream + branch - row_mean(branch)
    second_inverse = lax.rsqrt(row_mean(middle * middle) + EPSILON)
    second_unit = middle * second_inverse
    second_own = (second_unit * second_gain).astype(LOW)
    second_normed = jnp.concatenate([second_own, place.core_swap(second_own)], 0)
    hidden = dot(second_normed, hidden_full) + bias_h
    activated, gelu_pull = jax.vjp(
        lambda values_in: jax.nn.gelu(values_in, approximate=True), hidden
    )
    activated_low = activated.astype(LOW)
    hidden_grad = gelu_pull(dot(returned_grad, return_t))[0].astype(LOW)

    hidden_weight_grad = dot_tn(second_normed, hidden_grad)
    return_weight_grad = dot_tn(returned_grad, activated_low)
    step_h = place.half_step(place.split_rows(hidden_weight_grad), 1)
    step_r = place.shard_step(place.split_rows(return_weight_grad))
    activated_low = after(activated_low, hidden_weight_grad, return_weight_grad)
    returned_step = joined(dot_nt, activated_low, return_t)
    second_step = joined(dot_nt, after(hidden_grad, returned_step[0]), hidden_full)
    returned = added(returned_step, second_step[0]) + return_bias
    full_stream = middle + returned - row_mean(returned)
    result_own = full_stream.astype(LOW)
    result_far = place.tp_swap(result_own, 2)
    second_grad = added(second_step, result_own)

    second_scaled = second_grad * second_gain
    middle_grad = cot_full + second_inverse * (
        second_scaled - second_unit * row_mean(second_scaled * second_unit)
    )
    branch_own = (middle_grad - row_mean(middle_grad)).astype(LOW)
    branch_other = place.core_swap(branch_own)

    branch_grad = jnp.concatenate([branch_own, branch_other], 0)
    attended_grad = dot(branch_grad, exit_t).astype(LOW)
    far_dkv, inner, mixed = attend_far_back(meta, queries, far_kv, attended_grad, attended, logs)
    far_step = joined(dot_nt, far_dkv, weight_kv)
    result_pair = place.ordered(place.tp // 2, result_own, after(result_far, far_step[0]))
    result_near = place.tp_swap(result_pair, 1)
    exit_weight_grad = dot_tn(after(branch_grad, far_step[0]), attended)
    far_sum = added(far_step, exit_weight_grad).astype(LOW)
    far_grad = place.half_down(far_sum)
    step_h = place.shard_step(added(step_h, far_sum))
    step_r = place.half_step(added(step_r, far_sum), 0)
    query_low, near_dkv = attend_near_back(
        meta, queries, near_kv, attended_grad, logs, inner, after(mixed, result_pair, step_h[0], step_r[0])
    )
    sent = dot_nt(query_low[local:], weight_q) + dot_nt(near_dkv[local:], weight_kv)
    sent = sent.astype(LOW)
    query_kept, dkv_kept = after((query_low[:local], near_dkv[:local]), sent)
    kept = dot_nt(query_kept, weight_q) + dot_nt(dkv_kept, weight_kv)
    sum_h, sum_r = added(step_h, kept), added(step_r, kept)
    mlp_sent = jnp.concatenate([sum_h[:, units:], sum_r[:, units:]], 1).astype(LOW)
    mlp = (jnp.concatenate([sum_h[:, :units], sum_r[:, :units]], 1), place.tp_swap(mlp_sent, 1))
    first_grad = added((kept, place.core_swap(sent)), mlp_sent)
    first_grad = first_grad + after(far_grad, mlp_sent).astype(SINGLE)
    first_scaled = first_grad * first_gain
    stream_grad = middle_grad + first_inverse * (
        first_scaled - first_unit * row_mean(first_scaled * first_unit)
    )
    tokens_rows = (stream_grad - stream_grad[:, narrow:]).astype(LOW)
    tokens_far = place.tp_swap(tokens_rows, 2)

    normed_late = after(first_normed, tokens_rows)
    query_weight_grad = dot_tn(normed_late, query_low)
    kv_weight_grad = dot_tn(normed_late, near_dkv) + dot_tn(
        after(far_normed, tokens_rows), far_dkv
    )
    step_qe = place.shard_step(
        place.split_rows(jnp.concatenate([query_weight_grad, exit_weight_grad], 1))
    )
    step_kv = place.half_step(place.split_rows(kv_weight_grad), 1)
    mlp = added(mlp, step_kv[0], step_qe[0])
    tokens_pair = place.ordered(place.tp // 2, tokens_rows, after(tokens_far, mlp))
    tokens_near = place.tp_swap(tokens_pair, 1)
    mlp = place.block_step(after(mlp, tokens_pair))
    step_qe = place.half_step(added(step_qe, tokens_pair), 0)
    step_kv = place.shard_step(added(step_kv, tokens_pair))
    sums = jnp.concatenate([added(step_qe), added(step_kv)], 1)
    sums = [
        jnp.concatenate(
            [sums[:, at * width + low : at * width + low + head_width] for at in range(4)], 1
        )
        for low in (0, head_width)
    ]
    heads = place.tp_swap(after(sums[1].astype(LOW), tokens_near), 1)
    heads = place.block_step(added((sums[0], heads)))
    result = place.tp_all(result_pair, after(result_near, tokens_pair))[:, :, :narrow]
    mlp, heads = added(mlp, tokens_near), added(heads)
    tokens_grad = place.tp_all(tokens_pair, tokens_near)[:, :, :narrow]
    at = lambda index: heads[:, index * head_width : (index + 1) * head_width]
    entry_grad = jnp.stack([at(0), at(2), at(3)])
    exit_grad = at(1).T
    hidden_out = mlp[:, :units]
    return_out = mlp[:, units:].T

    return_bias_grad = jnp.sum(returned_own.astype(SINGLE), 0)
    exit_bias_grad = jnp.sum(branch_own.astype(SINGLE), 0)
    first_gain_grad = jnp.sum(first_grad * first_unit, 0)
    second_gain_grad = jnp.sum(second_grad * second_unit, 0)
    query_sum = jnp.sum(query_low.astype(SINGLE), 0).reshape(2, head_width)
    value_sum = jnp.sum(near_dkv[:, width:].astype(SINGLE), 0)
    value_sum = (value_sum + jnp.sum(far_dkv[:, width:].astype(SINGLE), 0)).reshape(2, head_width)
    hidden_sum = jnp.sum(hidden_grad.astype(SINGLE), 0).reshape(2, units)
    blocks = jnp.concatenate([query_sum, value_sum, hidden_sum], 1)
    first_id = jnp.where(place.home, place.tp, place.tp ^ 2)
    slots = []
    for slot in range(4):
        slots.append(
            jnp.where(first_id == slot, blocks[0], 0.0)
            + jnp.where(first_id == (slot ^ 1), blocks[1], 0.0)
        )
    vectors = jnp.concatenate(
        [first_gain_grad, exit_bias_grad, second_gain_grad, return_bias_grad] + slots
    )
    vectors = place.chip_total(after(vectors, tokens_pair))
    vectors = place.tp_total(after(vectors, tokens_near))
    own = lax.dynamic_index_in_dim(vectors[4 * wide :].reshape(4, -1), place.tp, 0, False)
    return (
        result,
        tokens_grad,
        vectors[:wide],
        entry_grad,
        own[:width].reshape(2, head_width),
        exit_grad,
        vectors[wide : 2 * wide],
        vectors[2 * wide : 3 * wide],
        hidden_out,
        own[width:],
        return_out,
        vectors[3 * wide : 4 * wide],
    )


def solution(mesh):
    return jax.shard_map(
        shards,
        mesh=mesh,
        in_specs=(
            P("shard", "ctx", None),
            P("shard"),
            P(),
            P(None, ("shard", "ctx"), "tp"),
            P(None, "tp"),
            P("tp", ("shard", "ctx")),
            P(),
            P(),
            P(("shard", "ctx"), "tp"),
            P("tp"),
            P("tp", ("shard", "ctx")),
            P(),
            P("shard", "ctx", None),
        ),
        out_specs=(
            P("shard", "ctx", None),
            P("shard", "ctx", None),
            P(),
            P(None, ("shard", "ctx"), "tp"),
            P(None, "tp"),
            P("tp", ("shard", "ctx")),
            P(),
            P(),
            P(("shard", "ctx"), "tp"),
            P("tp"),
            P("tp", ("shard", "ctx")),
            P(),
        ),
        check_vma=False,
    )
```

```python
import functools
import math

import jax
import jax.numpy as jnp
from jax import lax
from jax.experimental import pallas as pl
from jax.experimental.pallas import tpu as pltpu
from jax.sharding import PartitionSpec as P

HDIM = 64
PAIR = 2 * HDIM
EPSILON = 1e-05
MASKED = -1e30
LOW = jnp.bfloat16
SINGLE = jnp.float32


def row_mean(values):
    return jnp.mean(values, -1, keepdims=True)


def dot(left, right):
    return jnp.dot(left, right, preferred_element_type=SINGLE)


def dot_nt(left, right):
    return lax.dot_general(left, right, (((1,), (1,)), ((), ())), preferred_element_type=SINGLE)


def dot_tn(left, right):
    return lax.dot_general(left, right, (((0,), (0,)), ((), ())), preferred_element_type=SINGLE)


def key_positions(meta, block, local, upper):
    base = upper * 2 * local + (meta[1] ^ block) * local
    return base + lax.broadcasted_iota(jnp.int32, (local, 1), 0)


def query_positions(meta, block, local):
    base = meta[0] * 2 * local + (meta[1] ^ block) * local
    return base + lax.broadcasted_iota(jnp.int32, (1, local), 1)


def near_mask(meta, block, local):
    position = jnp.concatenate([key_positions(meta, b, local, meta[0]) for b in (0, 1)], 0)
    return (position <= query_positions(meta, block, local)) & (position < meta[2])


def far_mask(meta, local):
    position = jnp.concatenate([key_positions(meta, b, local, 0) for b in (0, 1)], 0)
    return position < jnp.where(meta[0] == 1, meta[2], 0)


def half_of(values, head):
    lanes = lax.broadcasted_iota(jnp.int32, values.shape, 1)
    return jnp.where(lanes // HDIM == head, values, jnp.zeros_like(values))


def each_head(local, body):
    @pl.loop(0, 4)
    def _(at):
        block, head = at // 2, at % 2
        body(block, head, pl.ds(pl.multiple_of(block * local, local), local), pl.ds(head, 1))


def prepare_kernel(
    meta, tokens_ref, cot_ref, gain_ref, stream_ref, unit_ref, inverse_ref, cot_out_ref, normed_ref,
    two_ref
):
    local, narrow = tokens_ref.shape
    inside = lax.broadcasted_iota(jnp.int32, (local, narrow + 1), 1) < narrow
    stream_ref[:, :narrow] = tokens_ref[...].astype(SINGLE)
    part = jnp.where(inside, stream_ref[...], 0.0)
    stream = jnp.where(inside, part, -jnp.sum(part, -1, keepdims=True))
    inverse = lax.rsqrt(row_mean(stream * stream) + EPSILON)
    unit = stream * inverse
    normed = (unit * gain_ref[...]).astype(LOW)
    stream_ref[...] = stream
    unit_ref[...] = unit
    inverse_ref[...] = inverse
    normed_ref[...] = normed
    two_ref[:, : narrow + 1] = normed
    position = meta[3] * local + lax.broadcasted_iota(jnp.int32, (local, 1), 0)
    cot_out_ref[:, :narrow] = cot_ref[...].astype(SINGLE)
    cot = jnp.where(inside & (position < meta[2]), cot_out_ref[...], 0.0)
    cot_out_ref[...] = cot
    two_ref[:, narrow + 1 :] = (cot - row_mean(cot)).astype(LOW)


def prepare(meta, tokens, cotangent, gain):
    local, narrow = tokens.shape
    wide = narrow + 1
    outs = [(wide, SINGLE), (wide, SINGLE), (1, SINGLE), (wide, SINGLE), (wide, LOW), (2 * wide, LOW)]
    own = pl.BlockSpec((local, narrow), lambda j, meta: (0, 0))
    return pl.pallas_call(
        prepare_kernel,
        grid_spec=pltpu.PrefetchScalarGridSpec(
            num_scalar_prefetch=1,
            grid=(1,),
            in_specs=[own, own, pl.BlockSpec((1, wide), lambda j, meta: (0, 0))],
            out_specs=[pl.BlockSpec((local, size), lambda j, meta: (0, 0)) for size, _ in outs],
        ),
        out_shape=[jax.ShapeDtypeStruct((local, size), dtype) for size, dtype in outs],
        cost_estimate=pl.CostEstimate(
            flops=20 * local * wide, bytes_accessed=20 * local * wide, transcendentals=local
        ),
        name="prepare",
    )(meta, tokens, cotangent, gain)


def forward_kernel(meta, q_ref, k_ref, v_ref, kf_ref, vf_ref, out_ref, log_ref, mix):
    local = q_ref.shape[0] // 2
    scale = jnp.asarray(1.0 / math.sqrt(HDIM), LOW)
    mix[...] = jnp.zeros_like(mix)

    def body(block, head, rows, line):
        near, far = near_mask(meta, block, local), far_mask(meta, local)
        query = half_of(q_ref[rows, :], head) * scale
        near_s = jnp.where(near, dot_nt(k_ref[...], query), MASKED)
        far_s = jnp.where(far, dot_nt(kf_ref[...], query), MASKED)
        top = jnp.maximum(jnp.max(near_s, 0, keepdims=True), jnp.max(far_s, 0, keepdims=True))
        near_p = jnp.exp(near_s - top)
        far_p = jnp.exp(far_s - top)
        total = jnp.sum(near_p, 0, keepdims=True) + jnp.sum(far_p, 0, keepdims=True)
        mixed = dot_tn(half_of(v_ref[...], head), near_p.astype(LOW))
        mixed = mixed + dot_tn(half_of(vf_ref[...], head), far_p.astype(LOW))
        mix[:, rows] += mixed / total
        log_ref[0, line, rows] = top + jnp.log(total)

    each_head(local, body)
    out_ref[...] = mix[...].T.astype(LOW)


def far_backward_kernel(
    meta, q_ref, k_ref, v_ref, grad_ref, out_ref, log_ref, dkv_ref, inner_ref, mix_ref, sums
):
    width = dkv_ref.shape[1] // 2
    local = q_ref.shape[0] // 2
    scale = jnp.asarray(1.0 / math.sqrt(HDIM), LOW)
    sums[...] = jnp.zeros_like(sums)
    mix_ref[...] = jnp.zeros_like(mix_ref)

    def body(block, head, rows, line):
        mask = far_mask(meta, local)
        query = half_of(q_ref[rows, :], head) * scale
        out_grad = half_of(grad_ref[rows, :], head)
        inner = out_grad.astype(SINGLE) * out_ref[rows, :].astype(SINGLE)
        inner = jnp.sum(inner.T, 0, keepdims=True)
        inner_ref[0, line, rows] = inner
        scores = jnp.where(mask, dot_nt(k_ref[...], query), MASKED)
        probs = jnp.exp(scores - log_ref[0, line, rows])
        grads = (probs * (dot_nt(v_ref[...], out_grad) - inner)).astype(LOW)
        sums[0] += dot(grads, query)
        sums[1] += dot(probs.astype(LOW), out_grad)
        mix_ref[0, :, rows] += dot_tn(half_of(k_ref[...], head), grads)

    each_head(local, body)
    lanes = pl.multiple_of(pl.program_id(0) * PAIR, PAIR)
    dkv_ref[:, pl.ds(lanes, PAIR)] = sums[0].astype(LOW)
    dkv_ref[:, pl.ds(width + lanes, PAIR)] = sums[1].astype(LOW)


def near_backward_kernel(
    meta, q_ref, k_ref, v_ref, grad_ref, log_ref, inner_ref, mix_ref, out_ref, sums, mix
):
    width = out_ref.shape[1] // 3
    local = q_ref.shape[0] // 2
    scale = 1.0 / math.sqrt(HDIM)
    sums[...] = jnp.zeros_like(sums)
    mix[...] = mix_ref[0]

    def body(block, head, rows, line):
        mask = near_mask(meta, block, local)
        query = half_of(q_ref[rows, :], head) * jnp.asarray(scale, LOW)
        out_grad = half_of(grad_ref[rows, :], head)
        scores = jnp.where(mask, dot_nt(k_ref[...], query), MASKED)
        probs = jnp.exp(scores - log_ref[0, line, rows])
        inner = inner_ref[0, line, rows]
        grads = (probs * (dot_nt(v_ref[...], out_grad) - inner)).astype(LOW)
        sums[0] += dot(grads, query)
        sums[1] += dot(probs.astype(LOW), out_grad)
        mix[:, rows] += dot_tn(half_of(k_ref[...], head), grads)

    each_head(local, body)
    lanes = pl.multiple_of(pl.program_id(0) * PAIR, PAIR)
    out_ref[:, pl.ds(lanes, PAIR)] = (mix[...] * scale).T.astype(LOW)
    out_ref[:, pl.ds(width + lanes, PAIR)] = sums[0].astype(LOW)
    out_ref[:, pl.ds(2 * width + lanes, PAIR)] = sums[1].astype(LOW)


def attention_call(kernel, name, meta, rows, width, operands, outs, scratch=()):
    pairs = width // PAIR
    part = lambda at: ((rows, PAIR), lambda j, meta: (0, at * pairs + j), (rows, width))
    specs = {
        0: part(0),
        1: part(1),
        2: part(2),
        "row": ((1, 2, rows), lambda j, meta: (j, 0, 0), (pairs, 2, rows)),
        "mix": ((1, PAIR, rows), lambda j, meta: (j, 0, 0), (pairs, PAIR, rows)),
        "two": ((rows, 2 * width), lambda j, meta: (0, 0), (rows, 2 * width)),
        "three": ((rows, 3 * width), lambda j, meta: (0, 0), (rows, 3 * width)),
    }
    return pl.pallas_call(
        kernel,
        grid_spec=pltpu.PrefetchScalarGridSpec(
            num_scalar_prefetch=1,
            grid=(pairs,),
            in_specs=[pl.BlockSpec(*specs[kind][:2]) for kind, _ in operands],
            out_specs=[pl.BlockSpec(*specs[kind][:2]) for kind, _ in outs],
            scratch_shapes=list(scratch),
        ),
        out_shape=[jax.ShapeDtypeStruct(specs[kind][2], dtype) for kind, dtype in outs],
        cost_estimate=pl.CostEstimate(
            flops=8 * rows * rows * width, bytes_accessed=rows * width * 16,
            transcendentals=rows * rows * width // HDIM,
        ),
        name=name,
    )(meta, *(array for _, array in operands))


def attend(meta, width, near, far_kv):
    return attention_call(
        forward_kernel, "attend", meta, near.shape[0], width,
        [(0, near), (1, near), (2, near), (0, far_kv), (1, far_kv)],
        [(0, LOW), ("row", SINGLE)],
        [pltpu.VMEM((PAIR, near.shape[0]), SINGLE)],
    )


def attend_far_back(meta, width, near, far_kv, grads, attended, logs):
    rows = near.shape[0]
    return attention_call(
        far_backward_kernel, "attend_far_back", meta, rows, width,
        [(0, near), (0, far_kv), (1, far_kv), (0, grads), (0, attended), ("row", logs)],
        [("two", LOW), ("row", SINGLE), ("mix", SINGLE)],
        [pltpu.VMEM((2, rows, PAIR), SINGLE)],
    )


def attend_near_back(meta, width, near, grads, logs, inner, mixed):
    rows = near.shape[0]
    return attention_call(
        near_backward_kernel, "attend_near_back", meta, rows, width,
        [(0, near), (1, near), (2, near), (0, grads), ("row", logs), ("row", inner),
         ("mix", mixed)],
        [("three", LOW)],
        [pltpu.VMEM((2, rows, PAIR), SINGLE), pltpu.VMEM((PAIR, rows), SINGLE)],
    )[0]


def after(value, *gates):
    return lax.optimization_barrier((value, *gates))[0]


class Place:
    def __init__(self):
        self.n_shard = lax.axis_size("shard")
        self.n_ctx = lax.axis_size("ctx")
        self.n_tp = lax.axis_size("tp")
        self.shard = lax.axis_index("shard")
        self.ctx = lax.axis_index("ctx")
        self.half = self.ctx // 2
        self.core = self.ctx % 2
        self.tp = lax.axis_index("tp")
        self.home = self.core == self.tp // 2

    def core_swap(self, value):
        return lax.ppermute(value, "ctx", [(i, i ^ 1) for i in range(self.n_ctx)])

    def half_swap(self, value):
        return lax.ppermute(value, "ctx", [(i, i ^ 2) for i in range(self.n_ctx)])

    def half_up(self, value):
        return lax.ppermute(value, "ctx", [(0, 2), (1, 3)])

    def half_down(self, value):
        return lax.ppermute(value, "ctx", [(2, 0), (3, 1)])

    def shard_swap(self, value):
        return lax.ppermute(value, "shard", [(0, 1), (1, 0)])

    def tp_swap(self, value, mask):
        return lax.ppermute(value, "tp", [(i, i ^ mask) for i in range(self.n_tp)])

    def ordered(self, flag, mine, other, axis=0):
        first = jnp.where(flag == 0, mine, other)
        second = jnp.where(flag == 0, other, mine)
        return jnp.stack([first, second], axis)


    def own_block(self, piece, far):
        kept = jnp.where(self.home, piece, far)
        sent = jnp.where(self.home, far, piece)
        return self.ordered(self.core, kept, self.core_swap(sent)).reshape(-1, piece.shape[1])

    def over_shards(self, value):
        if self.n_shard == 2:
            return self.ordered(self.shard, value, self.shard_swap(value))
        return lax.all_gather(value, "shard", axis=0)

    def rows_half_first(self, block):
        value = self.over_shards(self.ordered(self.half, block, self.half_swap(block)))
        return value.reshape(-1, block.shape[1])

    def rows_shard_first(self, block):
        value = self.over_shards(block)
        value = self.ordered(self.half, value, self.half_swap(value), 1)
        return value.reshape(-1, block.shape[1])


    def split_rows(self, value):
        rows, width = value.shape
        return value.reshape(self.n_shard, 2, rows // (2 * self.n_shard), width)

    def half_step(self, value, axis):
        sent = lax.dynamic_index_in_dim(value, 1 - self.half, axis, False).astype(LOW)
        kept = lax.dynamic_index_in_dim(value, self.half, axis, False)
        return kept, self.half_swap(sent), sent

    def shard_step(self, value):
        if self.n_shard == 2:
            sent = lax.dynamic_index_in_dim(value, 1 - self.shard, 0, False).astype(LOW)
            kept = lax.dynamic_index_in_dim(value, self.shard, 0, False)
            return kept, self.shard_swap(sent), sent
        kept = lax.psum_scatter(value, "shard", scatter_dimension=0, tiled=False)
        return kept, jnp.zeros_like(kept, LOW), kept

    def block_step(self, value):
        pieces = value.reshape(2, -1, value.shape[1])
        sent = lax.dynamic_index_in_dim(pieces, 1 - self.core, 0, False).astype(LOW)
        kept = lax.dynamic_index_in_dim(pieces, self.core, 0, False)
        got = self.core_swap(sent).astype(SINGLE)
        sent = jnp.where(self.home, got, kept).astype(LOW)
        return jnp.where(self.home, kept, got), self.tp_swap(sent, 2), sent

    def tp_all(self, pair, arriving):
        value = self.ordered(self.tp % 2, pair, arriving, 1)
        return value.reshape(4, *pair.shape[1:])

    def chip_total(self, value):
        value = value + self.core_swap(value)
        value = value + self.half_swap(value)
        if self.n_shard == 2:
            return value + self.shard_swap(value)
        return lax.psum(value, "shard")


def added(step, *gates):
    kept, arriving = step[:2]
    return kept + after(arriving, *gates).astype(SINGLE)


def interleaved(first, second, width):
    parts = []
    for start in range(0, first.shape[1], width):
        parts += [first[:, start : start + width], second[:, start : start + width]]
    return jnp.concatenate(parts, 1)


def shards(
    tokens,
    lengths,
    first_gain,
    entry_weight,
    entry_bias,
    exit_weight,
    exit_bias,
    second_gain,
    hidden_weight,
    hidden_bias,
    return_weight,
    return_bias,
    cotangent,
):
    place = Place()
    local, narrow = tokens.shape[1:]
    part = entry_weight.shape[1]
    head_width = entry_weight.shape[2]
    units = hidden_weight.shape[1]

    width = 2 * head_width

    piece_a = jnp.concatenate([entry_weight[1], entry_weight[2], entry_weight[0], exit_weight.T], 1)
    piece_b = jnp.concatenate([hidden_weight, return_weight.T], 1)
    biases = jnp.concatenate([entry_bias.reshape(-1), hidden_bias])
    far_a = place.tp_swap(piece_a, 2)
    bias_mine = jnp.where(place.home, biases, place.tp_swap(biases, 2))
    bias_two = jnp.stack([bias_mine, place.tp_swap(bias_mine, 1)])
    bias_q = bias_two[:, :head_width].reshape(-1)
    bias_v = bias_two[:, head_width:width].reshape(-1)
    bias_h = bias_two[:, width:].reshape(-1)
    mine_a = place.own_block(piece_a, far_a)
    other_a = place.tp_swap(mine_a, 1)

    wide = narrow + 1
    sequence = after(place.tp, other_a)
    length = lax.dynamic_index_in_dim(lengths, sequence, 0, False)
    meta = jnp.stack([place.half, place.core, length, place.ctx]).astype(jnp.int32)
    tokens_low, cot_low = (
        lax.dynamic_index_in_dim(item, sequence, 0, False) for item in (tokens, cotangent)
    )
    stream, first_unit, first_inverse, cot_full, normed_own, own_two = prepare(
        meta, tokens_low, cot_low, first_gain.reshape(1, wide)
    )
    far_own = place.half_up(normed_own)
    all_two = jnp.concatenate([own_two, place.core_swap(own_two)], 0)
    first_normed, returned_grad = all_two[:, :wide], all_two[:, wide:]

    block_kv = interleaved(mine_a[:, :width], other_a[:, :width], head_width)
    block_qe = interleaved(mine_a[:, width:], other_a[:, width:], head_width)
    half_kv = place.ordered(place.half, block_kv, place.half_swap(block_kv))
    weight_kv = place.over_shards(half_kv).reshape(-1, 2 * width)
    weight_qe = place.rows_shard_first(block_qe)
    exit_t = weight_qe[:, width:]
    weight_all = jnp.concatenate([weight_qe[:, :width], weight_kv], 1)
    piece_b = after(piece_b, other_a)
    mine_b = place.own_block(piece_b, place.tp_swap(piece_b, 2))
    other_b = place.tp_swap(mine_b, 1)

    far_own = after(far_own, weight_kv)
    far_normed = jnp.concatenate([far_own, place.core_swap(far_own)], 0)
    bias_all = jnp.concatenate([bias_q, jnp.zeros_like(bias_v), bias_v])
    block_h = jnp.concatenate([mine_b[:, :units], other_b[:, :units]], 1)
    block_r = jnp.concatenate([mine_b[:, units:], other_b[:, units:]], 1)
    block_h, block_r = after((block_h, block_r), weight_kv, weight_qe)
    half_h = place.ordered(place.half, block_h, place.half_swap(block_h))
    shard_r = place.over_shards(block_r)
    if place.n_shard == 2:
        last_h = place.shard_swap(half_h)
        hidden_full = place.ordered(place.shard, half_h, last_h)
    else:
        last_h = hidden_full = lax.all_gather(half_h, "shard")
    hidden_full = hidden_full.reshape(-1, 2 * units)
    last_r = place.half_swap(shard_r)
    return_t = place.ordered(place.half, shard_r, last_r, 1)
    return_t = return_t.reshape(-1, 2 * units)
    near = (dot(first_normed, weight_all) + bias_all).astype(LOW)
    far_kv = (dot(far_normed, weight_kv) + bias_all[width:]).astype(LOW)
    attended, logs = attend(meta, width, near, after(far_kv, half_h, shard_r))

    def joined(product, left, weight):
        sent = product(left[local:], weight).astype(LOW)
        return product(left[:local], weight), place.core_swap(sent)

    branch = added(joined(dot_nt, attended, exit_t), last_h, last_r) + exit_bias
    middle = stream + branch - row_mean(branch)
    second_inverse = lax.rsqrt(row_mean(middle * middle) + EPSILON)
    second_unit = middle * second_inverse
    second_own = (second_unit * second_gain).astype(LOW)
    second_normed = jnp.concatenate([second_own, place.core_swap(second_own)], 0)
    hidden = dot(second_normed, hidden_full) + bias_h
    activated, gelu_pull = jax.vjp(
        lambda values_in: jax.nn.gelu(values_in, approximate=True), hidden
    )
    activated_low = activated.astype(LOW)
    hidden_grad = gelu_pull(dot(returned_grad, return_t))[0].astype(LOW)

    returned_step = joined(dot_nt, activated_low, return_t)
    second_step = joined(dot_nt, after(hidden_grad, returned_step[0]), hidden_full)
    returned = added(returned_step, second_step[0]) + return_bias
    full_stream = middle + returned - row_mean(returned)
    result_own = full_stream.astype(LOW)
    result_far = place.tp_swap(result_own, 2)
    second_grad = added(second_step, result_own)

    second_scaled = second_grad * second_gain
    middle_grad = cot_full + second_inverse * (
        second_scaled - second_unit * row_mean(second_scaled * second_unit)
    )
    branch_own = (middle_grad - row_mean(middle_grad)).astype(LOW)
    branch_other = place.core_swap(branch_own)

    hidden_weight_grad = dot_tn(after(second_normed, branch_own), hidden_grad)
    return_weight_grad = dot_tn(returned_grad, after(activated_low, branch_own))
    step_h = place.half_step(place.split_rows(hidden_weight_grad), 1)
    step_r = place.shard_step(place.split_rows(return_weight_grad))

    branch_other = after(branch_other, step_h[2], step_r[2])
    branch_grad = jnp.concatenate([branch_own, branch_other], 0)
    attended_grad = dot(branch_grad, exit_t).astype(LOW)
    far_dkv, inner, mixed = attend_far_back(
        meta, width, near, far_kv, attended_grad, attended, logs
    )
    far_step = joined(dot_nt, far_dkv, weight_kv)
    exit_weight_grad = dot_tn(after(branch_grad, far_step[0]), attended)
    far_sum = added(far_step, exit_weight_grad).astype(LOW)
    far_grad = place.half_down(far_sum)
    result_pair = place.ordered(place.tp // 2, result_own, after(result_far, exit_weight_grad))
    result_near = place.tp_swap(result_pair, 1)
    mixed = after(mixed, far_sum, result_pair)
    grads = attend_near_back(meta, width, near, attended_grad, logs, inner, mixed)
    sent = dot_nt(grads[local:], weight_all).astype(LOW)
    kept = dot_nt(grads[:local], weight_all)
    sent = after(sent, result_near, far_grad)
    step_h = place.shard_step(added(step_h, kept))
    step_r = place.half_step(added(step_r, kept), 0)
    first_grad = added((kept, place.core_swap(sent)), step_h[2], step_r[2]) + far_grad.astype(SINGLE)
    first_scaled = first_grad * first_gain
    stream_grad = middle_grad + first_inverse * (
        first_scaled - first_unit * row_mean(first_scaled * first_unit)
    )
    tokens_rows = (stream_grad - stream_grad[:, narrow:]).astype(LOW)
    tokens_far = place.tp_swap(tokens_rows, 2)

    normed_late = after(first_normed, tokens_rows)
    grads = after(grads, tokens_rows)
    query_weight_grad = dot_tn(normed_late, grads[:, :width])
    kv_weight_grad = dot_tn(normed_late, grads[:, width:]) + dot_tn(
        after(far_normed, tokens_rows), far_dkv
    )
    sum_h, sum_r = added(step_h, kv_weight_grad), added(step_r, kv_weight_grad)
    mlp_sent = jnp.concatenate([sum_h[:, units:], sum_r[:, units:]], 1).astype(LOW)
    mlp = (jnp.concatenate([sum_h[:, :units], sum_r[:, :units]], 1), place.tp_swap(mlp_sent, 1))
    query_exit_grad = jnp.concatenate([query_weight_grad, exit_weight_grad], 1)
    step_qe = place.shard_step(place.split_rows(query_exit_grad))
    step_kv = place.half_step(place.split_rows(kv_weight_grad), 1)
    tokens_pair = place.ordered(
        place.tp // 2, tokens_rows, after(tokens_far, step_kv[2], step_qe[2])
    )
    tokens_near = place.tp_swap(tokens_pair, 1)
    mlp = place.block_step(added(mlp, tokens_pair))
    mlp_first = mlp[2]
    step_qe = place.half_step(added(step_qe, mlp_first), 0)
    step_kv = place.shard_step(added(step_kv, mlp_first))
    sums = jnp.concatenate([added(step_qe), added(step_kv)], 1)
    sums = [
        jnp.concatenate(
            [sums[:, at * width + low : at * width + low + head_width] for at in range(4)], 1
        )
        for low in (0, head_width)
    ]
    heads = added((sums[0], place.tp_swap(sums[1].astype(LOW), 1)), tokens_near)
    heads_sum = heads
    heads = place.block_step(heads)
    result = place.tp_all(result_pair, after(result_near, tokens_pair))[:, :, :narrow]
    mlp, heads = added(mlp, heads[0]), added(heads)
    tokens_grad = place.tp_all(tokens_pair, tokens_near)[:, :, :narrow]
    at = lambda index: heads[:, index * head_width : (index + 1) * head_width]
    entry_grad = jnp.stack([at(0), at(2), at(3)])
    exit_grad = at(1).T
    hidden_out = mlp[:, :units]
    return_out = mlp[:, units:].T

    return_bias_grad = jnp.sum(own_two[:, wide:].astype(SINGLE), 0)
    exit_bias_grad = jnp.sum(branch_own.astype(SINGLE), 0)
    first_gain_grad = jnp.sum(first_grad * first_unit, 0)
    second_gain_grad = jnp.sum(second_grad * second_unit, 0)
    query_sum = jnp.sum(grads[:, :width].astype(SINGLE), 0).reshape(2, head_width)
    value_sum = jnp.sum(grads[:, 2 * width :].astype(SINGLE), 0)
    value_sum = (value_sum + jnp.sum(far_dkv[:, width:].astype(SINGLE), 0)).reshape(2, head_width)
    hidden_sum = jnp.sum(hidden_grad.astype(SINGLE), 0).reshape(2, units)
    blocks = jnp.concatenate([query_sum, value_sum, hidden_sum], 1)
    first_id = jnp.where(place.home, place.tp, place.tp ^ 2)
    slots = []
    for slot in range(4):
        slots.append(
            jnp.where(first_id == slot, blocks[0], 0.0)
            + jnp.where(first_id == (slot ^ 1), blocks[1], 0.0)
        )
    pieces = [first_gain_grad, exit_bias_grad, second_gain_grad, return_bias_grad] + slots
    pieces = after(pieces, tokens_pair, mlp_sent)
    vectors = place.chip_total(after(jnp.concatenate(pieces), mlp_first))
    vectors = vectors + after(place.tp_swap(vectors, 1), heads_sum)
    vectors = vectors + place.tp_swap(vectors, 2)
    own = lax.dynamic_index_in_dim(vectors[4 * wide :].reshape(4, -1), place.tp, 0, False)
    return (
        result,
        tokens_grad,
        vectors[:wide],
        entry_grad,
        own[:width].reshape(2, head_width),
        exit_grad,
        vectors[wide : 2 * wide],
        vectors[2 * wide : 3 * wide],
        hidden_out,
        own[width:],
        return_out,
        vectors[3 * wide : 4 * wide],
    )


def solution(mesh):
    return jax.shard_map(
        shards,
        mesh=mesh,
        in_specs=(
            P("shard", "ctx", None),
            P("shard"),
            P(),
            P(None, ("shard", "ctx"), "tp"),
            P(None, "tp"),
            P("tp", ("shard", "ctx")),
            P(),
            P(),
            P(("shard", "ctx"), "tp"),
            P("tp"),
            P("tp", ("shard", "ctx")),
            P(),
            P("shard", "ctx", None),
        ),
        out_specs=(
            P("shard", "ctx", None),
            P("shard", "ctx", None),
            P(),
            P(None, ("shard", "ctx"), "tp"),
            P(None, "tp"),
            P("tp", ("shard", "ctx")),
            P(),
            P(),
            P(("shard", "ctx"), "tp"),
            P("tp"),
            P("tp", ("shard", "ctx")),
            P(),
        ),
        check_vma=False,
    )
```

```python
import functools
import math

import jax
import jax.numpy as jnp
from jax import lax
from jax.experimental import pallas as pl
from jax.experimental.pallas import tpu as pltpu
from jax.sharding import PartitionSpec as P

HDIM = 64
PAIR = 2 * HDIM
EPSILON = 1e-05
MASKED = -1e30
LOW = jnp.bfloat16
SINGLE = jnp.float32


def row_mean(values):
    return jnp.mean(values, -1, keepdims=True)


def dot(left, right):
    return jnp.dot(left, right, preferred_element_type=SINGLE)


def dot_nt(left, right):
    return lax.dot_general(left, right, (((1,), (1,)), ((), ())), preferred_element_type=SINGLE)


def dot_tn(left, right):
    return lax.dot_general(left, right, (((0,), (0,)), ((), ())), preferred_element_type=SINGLE)


def key_positions(meta, block, local, upper):
    base = upper * 2 * local + (meta[1] ^ block) * local
    return base + lax.broadcasted_iota(jnp.int32, (local, 1), 0)


def query_positions(meta, block, local):
    base = meta[0] * 2 * local + (meta[1] ^ block) * local
    return base + lax.broadcasted_iota(jnp.int32, (1, local), 1)


def near_mask(meta, block, local):
    position = jnp.concatenate([key_positions(meta, b, local, meta[0]) for b in (0, 1)], 0)
    return (position <= query_positions(meta, block, local)) & (position < meta[2])


def far_mask(meta, local):
    position = jnp.concatenate([key_positions(meta, b, local, 0) for b in (0, 1)], 0)
    return position < jnp.where(meta[0] == 1, meta[2], 0)


def half_of(values, head):
    lanes = lax.broadcasted_iota(jnp.int32, values.shape, 1)
    return jnp.where(lanes // HDIM == head, values, jnp.zeros_like(values))


def each_head(local, body):
    @pl.loop(0, 4)
    def _(at):
        block, head = at // 2, at % 2
        body(block, head, pl.ds(pl.multiple_of(block * local, local), local), pl.ds(head, 1))


def head_rows(head):
    return slice(head * HDIM, (head + 1) * HDIM)


def prepare_kernel(
    meta, tokens_ref, cot_ref, gain_ref, stream_ref, unit_ref, inverse_ref, cot_out_ref, normed_ref,
    two_ref
):
    local, narrow = tokens_ref.shape
    size = local // 4
    inside = lax.broadcasted_iota(jnp.int32, (size, narrow + 1), 1) < narrow

    @pl.loop(0, 4)
    def _(at):
        rows = pl.ds(pl.multiple_of(at * size, size), size)
        stream_ref[rows, :narrow] = tokens_ref[rows, :].astype(SINGLE)
        part = jnp.where(inside, stream_ref[rows, :], 0.0)
        stream = jnp.where(inside, part, -jnp.sum(part, -1, keepdims=True))
        inverse = lax.rsqrt(row_mean(stream * stream) + EPSILON)
        unit = stream * inverse
        normed = (unit * gain_ref[...]).astype(LOW)
        stream_ref[rows, :] = stream
        unit_ref[rows, :] = unit
        inverse_ref[rows, :] = inverse
        normed_ref[rows, :] = normed
        two_ref[rows, : narrow + 1] = normed
        position = lax.broadcasted_iota(jnp.int32, (size, 1), 0) + meta[3] * local + at * size
        cot_out_ref[rows, :narrow] = cot_ref[rows, :].astype(SINGLE)
        cot = jnp.where(inside & (position < meta[2]), cot_out_ref[rows, :], 0.0)
        cot_out_ref[rows, :] = cot
        two_ref[rows, narrow + 1 :] = (cot - row_mean(cot)).astype(LOW)


def prepare(meta, tokens, cotangent, gain):
    local, narrow = tokens.shape
    wide = narrow + 1
    outs = [(wide, SINGLE), (wide, SINGLE), (1, SINGLE), (wide, SINGLE), (wide, LOW), (2 * wide, LOW)]
    own = pl.BlockSpec((local, narrow), lambda j, meta: (0, 0))
    return pl.pallas_call(
        prepare_kernel,
        grid_spec=pltpu.PrefetchScalarGridSpec(
            num_scalar_prefetch=1,
            grid=(1,),
            in_specs=[own, own, pl.BlockSpec((1, wide), lambda j, meta: (0, 0))],
            out_specs=[pl.BlockSpec((local, size), lambda j, meta: (0, 0)) for size, _ in outs],
        ),
        out_shape=[jax.ShapeDtypeStruct((local, size), dtype) for size, dtype in outs],
        cost_estimate=pl.CostEstimate(
            flops=20 * local * wide, bytes_accessed=20 * local * wide, transcendentals=local
        ),
        name="prepare",
    )(meta, tokens, cotangent, gain)


def forward_kernel(meta, q_ref, k_ref, v_ref, kf_ref, vf_ref, out_ref, log_ref, mix):
    local = q_ref.shape[0] // 2
    scale = jnp.asarray(1.0 / math.sqrt(HDIM), LOW)
    mix[...] = jnp.zeros_like(mix)

    def body(block, head, rows, line):
        near, far = near_mask(meta, block, local), far_mask(meta, local)
        query = half_of(q_ref[rows, :], head) * scale
        near_s = jnp.where(near, dot_nt(k_ref[...], query), MASKED)
        far_s = jnp.where(far, dot_nt(kf_ref[...], query), MASKED)
        top = jnp.maximum(jnp.max(near_s, 0, keepdims=True), jnp.max(far_s, 0, keepdims=True))
        near_p = jnp.exp(near_s - top)
        far_p = jnp.exp(far_s - top)
        total = jnp.sum(near_p, 0, keepdims=True) + jnp.sum(far_p, 0, keepdims=True)
        mixed = dot_tn(half_of(v_ref[...], head), near_p.astype(LOW))
        mixed = mixed + dot_tn(half_of(vf_ref[...], head), far_p.astype(LOW))
        mix[:, rows] += mixed / total
        log_ref[0, line, rows] = top + jnp.log(total)

    each_head(local, body)
    out_ref[...] = mix[...].T.astype(LOW)


def far_backward_kernel(
    meta, q_ref, k_ref, v_ref, grad_ref, out_ref, log_ref, dkv_ref, inner_ref, mix_ref, sums
):
    rows_all, width = q_ref.shape[0], dkv_ref.shape[1] // 2
    local = rows_all // 2
    scale = jnp.asarray(1.0 / math.sqrt(HDIM), LOW)
    sums[...] = jnp.zeros_like(sums)

    @pl.loop(0, 2)
    def _(block):
        mask = far_mask(meta, local)
        rows = pl.ds(pl.multiple_of(block * local, local), local)
        product = (grad_ref[rows, :].astype(SINGLE) * out_ref[rows, :].astype(SINGLE)).T
        for head in (0, 1):
            query = half_of(q_ref[rows, :], head) * scale
            out_grad = half_of(grad_ref[rows, :], head)
            log_total = log_ref[0, head : head + 1, rows]
            inner = jnp.sum(product[head_rows(head)], 0, keepdims=True)
            inner_ref[0, head : head + 1, rows] = inner
            probs = jnp.exp(jnp.where(mask, dot_nt(k_ref[...], query), MASKED) - log_total)
            grads = (probs * (dot_nt(v_ref[...], out_grad) - inner)).astype(LOW)
            sums[0] += dot(grads, query)
            sums[1] += dot(probs.astype(LOW), out_grad)
            mix_ref[0, head_rows(head), rows] = dot_tn(k_ref[...], grads)[head_rows(head)]

    lanes = pl.multiple_of(pl.program_id(0) * PAIR, PAIR)
    dkv_ref[:, pl.ds(lanes, PAIR)] = sums[0].astype(LOW)
    dkv_ref[:, pl.ds(width + lanes, PAIR)] = sums[1].astype(LOW)


def near_backward_kernel(
    meta, q_ref, k_ref, v_ref, grad_ref, log_ref, inner_ref, mix_ref, out_ref, sums
):
    rows_all, width = q_ref.shape[0], out_ref.shape[1] // 3
    lanes = pl.multiple_of(pl.program_id(0) * PAIR, PAIR)
    local = rows_all // 2
    scale = 1.0 / math.sqrt(HDIM)
    sums[...] = jnp.zeros_like(sums)

    @pl.loop(0, 2)
    def _(block):
        mask = near_mask(meta, block, local)
        rows = pl.ds(pl.multiple_of(block * local, local), local)
        parts = []
        for head in (0, 1):
            query = half_of(q_ref[rows, :], head) * jnp.asarray(scale, LOW)
            out_grad = half_of(grad_ref[rows, :], head)
            log_total = log_ref[0, head : head + 1, rows]
            inner = inner_ref[0, head : head + 1, rows]
            probs = jnp.exp(jnp.where(mask, dot_nt(k_ref[...], query), MASKED) - log_total)
            grads = (probs * (dot_nt(v_ref[...], out_grad) - inner)).astype(LOW)
            sums[0] += dot(grads, query)
            sums[1] += dot(probs.astype(LOW), out_grad)
            mixed = dot_tn(k_ref[...], grads)[head_rows(head)]
            parts.append((mix_ref[0, head_rows(head), rows] + mixed) * scale)
        out_ref[rows, pl.ds(lanes, PAIR)] = jnp.concatenate(parts, 0).T.astype(LOW)

    out_ref[:, pl.ds(width + lanes, PAIR)] = sums[0].astype(LOW)
    out_ref[:, pl.ds(2 * width + lanes, PAIR)] = sums[1].astype(LOW)


def attention_call(kernel, name, meta, rows, width, operands, outs, scratch=()):
    pairs = width // PAIR
    part = lambda at: ((rows, PAIR), lambda j, meta: (0, at * pairs + j), (rows, width))
    specs = {
        0: part(0),
        1: part(1),
        2: part(2),
        "row": ((1, 2, rows), lambda j, meta: (j, 0, 0), (pairs, 2, rows)),
        "mix": ((1, PAIR, rows), lambda j, meta: (j, 0, 0), (pairs, PAIR, rows)),
        "two": ((rows, 2 * width), lambda j, meta: (0, 0), (rows, 2 * width)),
        "three": ((rows, 3 * width), lambda j, meta: (0, 0), (rows, 3 * width)),
    }
    return pl.pallas_call(
        kernel,
        grid_spec=pltpu.PrefetchScalarGridSpec(
            num_scalar_prefetch=1,
            grid=(pairs,),
            in_specs=[pl.BlockSpec(*specs[kind][:2]) for kind, _ in operands],
            out_specs=[pl.BlockSpec(*specs[kind][:2]) for kind, _ in outs],
            scratch_shapes=list(scratch),
        ),
        out_shape=[jax.ShapeDtypeStruct(specs[kind][2], dtype) for kind, dtype in outs],
        cost_estimate=pl.CostEstimate(
            flops=8 * rows * rows * width, bytes_accessed=rows * width * 16,
            transcendentals=rows * rows * width // HDIM,
        ),
        name=name,
    )(meta, *(array for _, array in operands))


def attend(meta, width, near, far_kv):
    return attention_call(
        forward_kernel, "attend", meta, near.shape[0], width,
        [(0, near), (1, near), (2, near), (0, far_kv), (1, far_kv)],
        [(0, LOW), ("row", SINGLE)],
        [pltpu.VMEM((PAIR, near.shape[0]), SINGLE)],
    )


def attend_far_back(meta, width, near, far_kv, grads, attended, logs):
    rows = near.shape[0]
    return attention_call(
        far_backward_kernel, "attend_far_back", meta, rows, width,
        [(0, near), (0, far_kv), (1, far_kv), (0, grads), (0, attended), ("row", logs)],
        [("two", LOW), ("row", SINGLE), ("mix", SINGLE)],
        [pltpu.VMEM((2, rows, PAIR), SINGLE)],
    )


def attend_near_back(meta, width, near, grads, logs, inner, mixed):
    rows = near.shape[0]
    return attention_call(
        near_backward_kernel, "attend_near_back", meta, rows, width,
        [(0, near), (1, near), (2, near), (0, grads), ("row", logs), ("row", inner),
         ("mix", mixed)],
        [("three", LOW)],
        [pltpu.VMEM((2, rows, PAIR), SINGLE)],
    )[0]


def after(value, *gates):
    return lax.optimization_barrier((value, *gates))[0]


class Place:
    def __init__(self):
        self.n_shard = lax.axis_size("shard")
        self.n_ctx = lax.axis_size("ctx")
        self.n_tp = lax.axis_size("tp")
        self.shard = lax.axis_index("shard")
        self.ctx = lax.axis_index("ctx")
        self.half = self.ctx // 2
        self.core = self.ctx % 2
        self.tp = lax.axis_index("tp")
        self.home = self.core == self.tp // 2

    def core_swap(self, value):
        return lax.ppermute(value, "ctx", [(i, i ^ 1) for i in range(self.n_ctx)])

    def half_swap(self, value):
        return lax.ppermute(value, "ctx", [(i, i ^ 2) for i in range(self.n_ctx)])

    def half_up(self, value):
        return lax.ppermute(value, "ctx", [(0, 2), (1, 3)])

    def half_down(self, value):
        return lax.ppermute(value, "ctx", [(2, 0), (3, 1)])

    def shard_swap(self, value):
        return lax.ppermute(value, "shard", [(0, 1), (1, 0)])

    def tp_swap(self, value, mask):
        return lax.ppermute(value, "tp", [(i, i ^ mask) for i in range(self.n_tp)])

    def ordered(self, flag, mine, other, axis=0):
        first = jnp.where(flag == 0, mine, other)
        second = jnp.where(flag == 0, other, mine)
        return jnp.stack([first, second], axis)


    def own_block(self, piece, far):
        kept = jnp.where(self.home, piece, far)
        sent = jnp.where(self.home, far, piece)
        return self.ordered(self.core, kept, self.core_swap(sent)).reshape(-1, piece.shape[1])

    def over_shards(self, value):
        if self.n_shard == 2:
            return self.ordered(self.shard, value, self.shard_swap(value))
        return lax.all_gather(value, "shard", axis=0)

    def rows_half_first(self, block):
        value = self.over_shards(self.ordered(self.half, block, self.half_swap(block)))
        return value.reshape(-1, block.shape[1])

    def rows_shard_first(self, block):
        value = self.over_shards(block)
        value = self.ordered(self.half, value, self.half_swap(value), 1)
        return value.reshape(-1, block.shape[1])


    def split_rows(self, value):
        rows, width = value.shape
        return value.reshape(self.n_shard, 2, rows // (2 * self.n_shard), width)

    def step(self, values, index, axis, swap):
        pick = lambda value, at: lax.dynamic_index_in_dim(value, at, axis, False)
        sent = [pick(value, 1 - index).astype(LOW) for value in values]
        sent = jnp.concatenate(sent, -1) if len(sent) > 1 else sent[0]
        got, steps, start = swap(sent), [], 0
        for value in values:
            stop = start + value.shape[-1]
            steps.append((pick(value, index), got[..., start:stop], sent))
            start = stop
        return steps

    def half_steps(self, values, axis):
        return self.step(values, self.half, axis, self.half_swap)

    def half_step(self, value, axis):
        return self.half_steps([value], axis)[0]

    def shard_steps(self, values):
        if self.n_shard == 2:
            return self.step(values, self.shard, 0, self.shard_swap)
        kept = [
            lax.psum_scatter(value, "shard", scatter_dimension=0, tiled=False) for value in values
        ]
        return [(value, jnp.zeros_like(value, LOW), value) for value in kept]

    def shard_step(self, value):
        return self.shard_steps([value])[0]

    def block_step(self, value):
        pieces = value.reshape(2, -1, value.shape[1])
        sent = lax.dynamic_index_in_dim(pieces, 1 - self.core, 0, False).astype(LOW)
        kept = lax.dynamic_index_in_dim(pieces, self.core, 0, False)
        got = self.core_swap(sent).astype(SINGLE)
        sent = jnp.where(self.home, got, kept).astype(LOW)
        return jnp.where(self.home, kept, got), self.tp_swap(sent, 2), sent

    def tp_all(self, pair, arriving):
        value = self.ordered(self.tp % 2, pair, arriving, 1)
        return value.reshape(4, *pair.shape[1:])

    def chip_total(self, value):
        value = value + self.core_swap(value)
        value = value + self.half_swap(value)
        if self.n_shard == 2:
            return value + self.shard_swap(value)
        return lax.psum(value, "shard")


def added(step, *gates):
    kept, arriving = step[:2]
    return kept + after(arriving, *gates).astype(SINGLE)


def interleaved(first, second, width):
    parts = []
    for start in range(0, first.shape[1], width):
        parts += [first[:, start : start + width], second[:, start : start + width]]
    return jnp.concatenate(parts, 1)


def shards(
    tokens,
    lengths,
    first_gain,
    entry_weight,
    entry_bias,
    exit_weight,
    exit_bias,
    second_gain,
    hidden_weight,
    hidden_bias,
    return_weight,
    return_bias,
    cotangent,
):
    place = Place()
    local, narrow = tokens.shape[1:]
    part = entry_weight.shape[1]
    head_width = entry_weight.shape[2]
    units = hidden_weight.shape[1]

    width = 2 * head_width

    piece_a = jnp.concatenate([entry_weight[1], entry_weight[2], entry_weight[0], exit_weight.T], 1)
    piece_b = jnp.concatenate([hidden_weight, return_weight.T], 1)
    biases = jnp.concatenate([entry_bias.reshape(-1), hidden_bias])
    far_a = place.tp_swap(piece_a, 2)
    bias_mine = jnp.where(place.home, biases, place.tp_swap(biases, 2))
    bias_two = jnp.stack([bias_mine, place.tp_swap(bias_mine, 1)])
    bias_q = bias_two[:, :head_width].reshape(-1)
    bias_v = bias_two[:, head_width:width].reshape(-1)
    bias_h = bias_two[:, width:].reshape(-1)
    mine_a = place.own_block(piece_a, far_a)
    other_a = place.tp_swap(mine_a, 1)

    wide = narrow + 1
    sequence = after(place.tp, other_a)
    length = lax.dynamic_index_in_dim(lengths, sequence, 0, False)
    meta = jnp.stack([place.half, place.core, length, place.ctx]).astype(jnp.int32)
    tokens_low = lax.dynamic_index_in_dim(tokens, sequence, 0, False)
    cot_low = lax.dynamic_index_in_dim(cotangent, after(sequence, tokens_low), 0, False)
    stream, first_unit, first_inverse, cot_full, normed_own, own_two = prepare(
        meta, tokens_low, cot_low, first_gain.reshape(1, wide)
    )
    far_own = place.half_up(normed_own)
    all_two = jnp.concatenate([own_two, place.core_swap(own_two)], 0)
    first_normed, returned_grad = all_two[:, :wide], all_two[:, wide:]

    block_kv = interleaved(mine_a[:, :width], other_a[:, :width], head_width)
    block_qe = interleaved(mine_a[:, width:], other_a[:, width:], head_width)
    half_kv = place.ordered(place.half, block_kv, place.half_swap(block_kv))
    weight_kv = place.over_shards(half_kv).reshape(-1, 2 * width)
    weight_qe = place.rows_shard_first(block_qe)
    exit_t = weight_qe[:, width:]
    weight_all = jnp.concatenate([weight_qe[:, :width], weight_kv], 1)
    piece_b = after(piece_b, other_a)
    mine_b = place.own_block(piece_b, place.tp_swap(piece_b, 2))
    other_b = place.tp_swap(mine_b, 1)

    far_own = after(far_own, weight_kv)
    far_normed = jnp.concatenate([far_own, place.core_swap(far_own)], 0)
    bias_all = jnp.concatenate([bias_q, jnp.zeros_like(bias_v), bias_v])
    block_h = jnp.concatenate([mine_b[:, :units], other_b[:, :units]], 1)
    block_r = jnp.concatenate([mine_b[:, units:], other_b[:, units:]], 1)
    block_h, block_r = after((block_h, block_r), weight_kv, weight_qe)
    half_h = place.ordered(place.half, block_h, place.half_swap(block_h))
    shard_r = place.over_shards(block_r)
    if place.n_shard == 2:
        last_h = place.shard_swap(half_h)
        hidden_full = place.ordered(place.shard, half_h, last_h)
    else:
        last_h = hidden_full = lax.all_gather(half_h, "shard")
    hidden_full = hidden_full.reshape(-1, 2 * units)
    last_r = place.half_swap(shard_r)
    return_t = place.ordered(place.half, shard_r, last_r, 1)
    return_t = return_t.reshape(-1, 2 * units)
    near = (dot(first_normed, weight_all) + bias_all).astype(LOW)
    far_kv = (dot(far_normed, weight_kv) + bias_all[width:]).astype(LOW)
    attended, logs = attend(meta, width, near, after(far_kv, half_h, shard_r))

    def joined(product, left, weight):
        sent = product(left[local:], weight).astype(LOW)
        return product(left[:local], weight), place.core_swap(sent)

    branch = added(joined(dot_nt, attended, exit_t), last_h, last_r) + exit_bias
    middle = stream + branch - row_mean(branch)
    second_inverse = lax.rsqrt(row_mean(middle * middle) + EPSILON)
    second_unit = middle * second_inverse
    second_own = (second_unit * second_gain).astype(LOW)
    second_normed = jnp.concatenate([second_own, place.core_swap(second_own)], 0)
    hidden = dot(second_normed, hidden_full) + bias_h
    activated, gelu_pull = jax.vjp(
        lambda values_in: jax.nn.gelu(values_in, approximate=True), hidden
    )
    activated_low = activated.astype(LOW)
    hidden_grad = gelu_pull(dot(returned_grad, return_t))[0].astype(LOW)

    returned_step = joined(dot_nt, activated_low, return_t)
    second_step = joined(dot_nt, after(hidden_grad, returned_step[0]), hidden_full)
    returned = added(returned_step, second_step[0]) + return_bias
    full_stream = middle + returned - row_mean(returned)
    result_own = full_stream.astype(LOW)
    result_far = place.tp_swap(result_own, 2)
    second_grad = added(second_step, result_own)

    second_scaled = second_grad * second_gain
    middle_grad = cot_full + second_inverse * (
        second_scaled - second_unit * row_mean(second_scaled * second_unit)
    )
    branch_own = (middle_grad - row_mean(middle_grad)).astype(LOW)
    branch_other = place.core_swap(branch_own)

    hidden_weight_grad = dot_tn(after(second_normed, branch_own), hidden_grad)
    return_weight_grad = dot_tn(returned_grad, after(activated_low, branch_own))
    step_h = place.half_step(place.split_rows(hidden_weight_grad), 1)
    step_r = place.shard_step(place.split_rows(return_weight_grad))

    branch_other = after(branch_other, step_h[2], step_r[2])
    branch_grad = jnp.concatenate([branch_own, branch_other], 0)
    attended_grad = dot(branch_grad, exit_t).astype(LOW)
    far_dkv, inner, mixed = attend_far_back(
        meta, width, near, far_kv, attended_grad, attended, logs
    )
    far_step = joined(dot_nt, far_dkv, weight_kv)
    exit_weight_grad = dot_tn(after(branch_grad, far_step[0]), attended)
    far_sum = added(far_step, exit_weight_grad).astype(LOW)
    far_grad = place.half_down(far_sum)
    result_pair = place.ordered(place.tp // 2, result_own, after(result_far, exit_weight_grad))
    result_near = place.tp_swap(result_pair, 1)
    mixed = after(mixed, far_sum, result_pair)
    grads = attend_near_back(meta, width, near, attended_grad, logs, inner, mixed)
    sent = dot_nt(grads[local:], weight_all).astype(LOW)
    kept = dot_nt(grads[:local], weight_all)
    sent = after(sent, result_near, far_grad)
    step_h = place.shard_step(added(step_h, kept))
    step_r = place.half_step(added(step_r, kept), 0)
    first_grad = added((kept, place.core_swap(sent)), step_h[2], step_r[2]) + far_grad.astype(SINGLE)
    first_scaled = first_grad * first_gain
    stream_grad = middle_grad + first_inverse * (
        first_scaled - first_unit * row_mean(first_scaled * first_unit)
    )
    tokens_rows = (stream_grad - stream_grad[:, narrow:]).astype(LOW)
    tokens_far = place.tp_swap(tokens_rows, 2)

    normed_late = after(first_normed, tokens_rows)
    grads = after(grads, tokens_rows)
    query_weight_grad = dot_tn(normed_late, grads[:, :width])
    kv_weight_grad = dot_tn(normed_late, grads[:, width:]) + dot_tn(
        after(far_normed, tokens_rows), far_dkv
    )
    sum_h, sum_r = added(step_h, kv_weight_grad), added(step_r, kv_weight_grad)
    mlp_sent = jnp.concatenate([sum_h[:, units:], sum_r[:, units:]], 1).astype(LOW)
    mlp = (jnp.concatenate([sum_h[:, :units], sum_r[:, :units]], 1), place.tp_swap(mlp_sent, 1))
    step_q, step_e = place.shard_steps(
        [place.split_rows(query_weight_grad), place.split_rows(exit_weight_grad)]
    )
    step_kv = place.half_step(place.split_rows(kv_weight_grad), 1)
    tokens_pair = place.ordered(
        place.tp // 2, tokens_rows, after(tokens_far, step_kv[2], step_q[2])
    )
    tokens_near = place.tp_swap(tokens_pair, 1)
    result = place.tp_all(result_pair, after(result_near, tokens_pair))[:, :, :narrow]
    mlp = place.block_step(added(mlp, tokens_pair, result))
    mlp_first = mlp[2]
    step_q, step_e = place.half_steps(
        [added(step_q, mlp_first), added(step_e, mlp_first)], 0
    )
    step_kv = place.shard_step(added(step_kv, mlp_first))
    sums, sum_kv = [added(step_q), added(step_e)], added(step_kv)
    sums += [sum_kv[:, :width], sum_kv[:, width:]]
    sums = [
        jnp.concatenate([value[:, low : low + head_width] for value in sums], 1)
        for low in (0, head_width)
    ]
    heads = place.tp_swap(after(sums[1].astype(LOW), mlp[1]), 1)
    heads = added((sums[0], heads), tokens_near)
    heads_sum = heads
    heads = place.block_step(heads)
    tokens_grad = place.tp_all(tokens_pair, after(tokens_near, heads[2]))[:, :, :narrow]
    mlp, heads = added(mlp, heads[0]), added(heads)
    at = lambda index: heads[:, index * head_width : (index + 1) * head_width]
    entry_grad = jnp.stack([at(0), at(2), at(3)])
    exit_grad = at(1).T
    hidden_out = mlp[:, :units]
    return_out = mlp[:, units:].T

    return_bias_grad = jnp.sum(own_two[:, wide:].astype(SINGLE), 0)
    exit_bias_grad = jnp.sum(branch_own.astype(SINGLE), 0)
    first_gain_grad = jnp.sum(first_grad * first_unit, 0)
    second_gain_grad = jnp.sum(second_grad * second_unit, 0)
    query_sum = jnp.sum(grads[:, :width].astype(SINGLE), 0).reshape(2, head_width)
    value_sum = jnp.sum(grads[:, 2 * width :].astype(SINGLE), 0)
    value_sum = (value_sum + jnp.sum(far_dkv[:, width:].astype(SINGLE), 0)).reshape(2, head_width)
    hidden_sum = jnp.sum(hidden_grad.astype(SINGLE), 0).reshape(2, units)
    blocks = jnp.concatenate([query_sum, value_sum, hidden_sum], 1)
    first_id = jnp.where(place.home, place.tp, place.tp ^ 2)
    slots = []
    for slot in range(4):
        slots.append(
            jnp.where(first_id == slot, blocks[0], 0.0)
            + jnp.where(first_id == (slot ^ 1), blocks[1], 0.0)
        )
    pieces = [first_gain_grad, exit_bias_grad, second_gain_grad, return_bias_grad] + slots
    pieces = after(pieces, tokens_pair, mlp_sent)
    vectors = place.chip_total(after(jnp.concatenate(pieces), mlp_first))
    vectors = vectors + after(place.tp_swap(vectors, 1), heads_sum)
    vectors = vectors + place.tp_swap(vectors, 2)
    own = lax.dynamic_index_in_dim(vectors[4 * wide :].reshape(4, -1), place.tp, 0, False)
    return (
        result,
        tokens_grad,
        vectors[:wide],
        entry_grad,
        own[:width].reshape(2, head_width),
        exit_grad,
        vectors[wide : 2 * wide],
        vectors[2 * wide : 3 * wide],
        hidden_out,
        own[width:],
        return_out,
        vectors[3 * wide : 4 * wide],
    )


def solution(mesh):
    return jax.shard_map(
        shards,
        mesh=mesh,
        in_specs=(
            P("shard", "ctx", None),
            P("shard"),
            P(),
            P(None, ("shard", "ctx"), "tp"),
            P(None, "tp"),
            P("tp", ("shard", "ctx")),
            P(),
            P(),
            P(("shard", "ctx"), "tp"),
            P("tp"),
            P("tp", ("shard", "ctx")),
            P(),
            P("shard", "ctx", None),
        ),
        out_specs=(
            P("shard", "ctx", None),
            P("shard", "ctx", None),
            P(),
            P(None, ("shard", "ctx"), "tp"),
            P(None, "tp"),
            P("tp", ("shard", "ctx")),
            P(),
            P(),
            P(("shard", "ctx"), "tp"),
            P("tp"),
            P("tp", ("shard", "ctx")),
            P(),
        ),
        check_vma=False,
    )
```

```python
import functools
import math

import jax
import jax.numpy as jnp
from jax import lax
from jax.experimental import pallas as pl
from jax.experimental.pallas import tpu as pltpu
from jax.sharding import PartitionSpec as P

HDIM = 64
PAIR = 2 * HDIM
EPSILON = 1e-05
MASKED = -1e30
LOW = jnp.bfloat16
SINGLE = jnp.float32


def row_mean(values):
    return jnp.mean(values, -1, keepdims=True)


def dot(left, right):
    return jnp.dot(left, right, preferred_element_type=SINGLE)


def dot_nt(left, right):
    return lax.dot_general(left, right, (((1,), (1,)), ((), ())), preferred_element_type=SINGLE)


def dot_tn(left, right):
    return lax.dot_general(left, right, (((0,), (0,)), ((), ())), preferred_element_type=SINGLE)


def key_positions(meta, block, local, upper):
    base = upper * 2 * local + (meta[1] ^ block) * local
    return base + lax.broadcasted_iota(jnp.int32, (local, 1), 0)


def query_positions(meta, block, local):
    base = meta[0] * 2 * local + (meta[1] ^ block) * local
    return base + lax.broadcasted_iota(jnp.int32, (1, local), 1)


def near_mask(meta, block, local):
    position = jnp.concatenate([key_positions(meta, b, local, meta[0]) for b in (0, 1)], 0)
    return (position <= query_positions(meta, block, local)) & (position < meta[2])


def far_mask(meta, local):
    position = jnp.concatenate([key_positions(meta, b, local, 0) for b in (0, 1)], 0)
    return position < jnp.where(meta[0] == 1, meta[2], 0)


def half_of(values, head):
    lanes = lax.broadcasted_iota(jnp.int32, values.shape, 1)
    return jnp.where(lanes // HDIM == head, values, jnp.zeros_like(values))


def each_head(local, body):
    @pl.loop(0, 4)
    def _(at):
        block, head = at // 2, at % 2
        body(block, head, pl.ds(pl.multiple_of(block * local, local), local), pl.ds(head, 1))


def head_rows(head):
    return slice(head * HDIM, (head + 1) * HDIM)


def prepare_kernel(
    meta, tokens_ref, cot_ref, gain_ref, stream_ref, unit_ref, inverse_ref, cot_out_ref, normed_ref,
    two_ref
):
    local, narrow = tokens_ref.shape
    size = local // 4
    inside = lax.broadcasted_iota(jnp.int32, (size, narrow + 1), 1) < narrow

    @pl.loop(0, 4)
    def _(at):
        rows = pl.ds(pl.multiple_of(at * size, size), size)
        stream_ref[rows, :narrow] = tokens_ref[rows, :].astype(SINGLE)
        part = jnp.where(inside, stream_ref[rows, :], 0.0)
        stream = jnp.where(inside, part, -jnp.sum(part, -1, keepdims=True))
        inverse = lax.rsqrt(row_mean(stream * stream) + EPSILON)
        unit = stream * inverse
        normed = (unit * gain_ref[...]).astype(LOW)
        stream_ref[rows, :] = stream
        unit_ref[rows, :] = unit
        inverse_ref[rows, :] = inverse
        normed_ref[rows, :] = normed
        two_ref[rows, : narrow + 1] = normed
        position = lax.broadcasted_iota(jnp.int32, (size, 1), 0) + meta[3] * local + at * size
        cot_out_ref[rows, :narrow] = cot_ref[rows, :].astype(SINGLE)
        cot = jnp.where(inside & (position < meta[2]), cot_out_ref[rows, :], 0.0)
        cot_out_ref[rows, :] = cot
        two_ref[rows, narrow + 1 :] = (cot - row_mean(cot)).astype(LOW)


def prepare(meta, tokens, cotangent, gain):
    local, narrow = tokens.shape
    wide = narrow + 1
    outs = [(wide, SINGLE), (wide, SINGLE), (1, SINGLE), (wide, SINGLE), (wide, LOW), (2 * wide, LOW)]
    own = pl.BlockSpec((local, narrow), lambda j, meta: (0, 0))
    return pl.pallas_call(
        prepare_kernel,
        grid_spec=pltpu.PrefetchScalarGridSpec(
            num_scalar_prefetch=1,
            grid=(1,),
            in_specs=[own, own, pl.BlockSpec((1, wide), lambda j, meta: (0, 0))],
            out_specs=[pl.BlockSpec((local, size), lambda j, meta: (0, 0)) for size, _ in outs],
        ),
        out_shape=[jax.ShapeDtypeStruct((local, size), dtype) for size, dtype in outs],
        cost_estimate=pl.CostEstimate(
            flops=20 * local * wide, bytes_accessed=20 * local * wide, transcendentals=local
        ),
        name="prepare",
    )(meta, tokens, cotangent, gain)


def forward_kernel(meta, q_ref, k_ref, v_ref, kf_ref, vf_ref, out_ref, log_ref, mix):
    local = q_ref.shape[0] // 2
    scale = jnp.asarray(1.0 / math.sqrt(HDIM), LOW)
    mix[...] = jnp.zeros_like(mix)

    def body(block, head, rows, line):
        near, far = near_mask(meta, block, local), far_mask(meta, local)
        query = half_of(q_ref[rows, :], head) * scale
        near_s = jnp.where(near, dot_nt(k_ref[...], query), MASKED)
        far_s = jnp.where(far, dot_nt(kf_ref[...], query), MASKED)
        top = jnp.maximum(jnp.max(near_s, 0, keepdims=True), jnp.max(far_s, 0, keepdims=True))
        near_p = jnp.exp(near_s - top)
        far_p = jnp.exp(far_s - top)
        total = jnp.sum(near_p, 0, keepdims=True) + jnp.sum(far_p, 0, keepdims=True)
        mixed = dot_tn(half_of(v_ref[...], head), near_p.astype(LOW))
        mixed = mixed + dot_tn(half_of(vf_ref[...], head), far_p.astype(LOW))
        mix[:, rows] += mixed / total
        log_ref[0, line, rows] = top + jnp.log(total)

    each_head(local, body)
    out_ref[...] = mix[...].T.astype(LOW)


def far_backward_kernel(
    meta, q_ref, k_ref, v_ref, grad_ref, out_ref, log_ref, dkv_ref, inner_ref, mix_ref, sums
):
    rows_all, width = q_ref.shape[0], dkv_ref.shape[1] // 2
    local = rows_all // 2
    scale = jnp.asarray(1.0 / math.sqrt(HDIM), LOW)
    sums[...] = jnp.zeros_like(sums)

    @pl.loop(0, 2)
    def _(block):
        mask = far_mask(meta, local)
        rows = pl.ds(pl.multiple_of(block * local, local), local)
        product = (grad_ref[rows, :].astype(SINGLE) * out_ref[rows, :].astype(SINGLE)).T
        for head in (0, 1):
            query = half_of(q_ref[rows, :], head) * scale
            out_grad = half_of(grad_ref[rows, :], head)
            log_total = log_ref[0, head : head + 1, rows]
            inner = jnp.sum(product[head_rows(head)], 0, keepdims=True)
            inner_ref[0, head : head + 1, rows] = inner
            probs = jnp.exp(jnp.where(mask, dot_nt(k_ref[...], query), MASKED) - log_total)
            grads = (probs * (dot_nt(v_ref[...], out_grad) - inner)).astype(LOW)
            sums[0] += dot(grads, query)
            sums[1] += dot(probs.astype(LOW), out_grad)
            mix_ref[0, head_rows(head), rows] = dot_tn(k_ref[...], grads)[head_rows(head)]

    lanes = pl.multiple_of(pl.program_id(0) * PAIR, PAIR)
    dkv_ref[:, pl.ds(lanes, PAIR)] = sums[0].astype(LOW)
    dkv_ref[:, pl.ds(width + lanes, PAIR)] = sums[1].astype(LOW)


def near_backward_kernel(
    meta, q_ref, k_ref, v_ref, grad_ref, log_ref, inner_ref, mix_ref, out_ref, sums
):
    rows_all, width = q_ref.shape[0], out_ref.shape[1] // 3
    lanes = pl.multiple_of(pl.program_id(0) * PAIR, PAIR)
    local = rows_all // 2
    scale = 1.0 / math.sqrt(HDIM)
    sums[...] = jnp.zeros_like(sums)

    @pl.loop(0, 2)
    def _(block):
        mask = near_mask(meta, block, local)
        rows = pl.ds(pl.multiple_of(block * local, local), local)
        parts = []
        for head in (0, 1):
            query = half_of(q_ref[rows, :], head) * jnp.asarray(scale, LOW)
            out_grad = half_of(grad_ref[rows, :], head)
            log_total = log_ref[0, head : head + 1, rows]
            inner = inner_ref[0, head : head + 1, rows]
            probs = jnp.exp(jnp.where(mask, dot_nt(k_ref[...], query), MASKED) - log_total)
            grads = (probs * (dot_nt(v_ref[...], out_grad) - inner)).astype(LOW)
            sums[0] += dot(grads, query)
            sums[1] += dot(probs.astype(LOW), out_grad)
            mixed = dot_tn(k_ref[...], grads)[head_rows(head)]
            parts.append((mix_ref[0, head_rows(head), rows] + mixed) * scale)
        out_ref[rows, pl.ds(lanes, PAIR)] = jnp.concatenate(parts, 0).T.astype(LOW)

    out_ref[:, pl.ds(width + lanes, PAIR)] = sums[0].astype(LOW)
    out_ref[:, pl.ds(2 * width + lanes, PAIR)] = sums[1].astype(LOW)


def attention_call(kernel, name, meta, rows, width, operands, outs, scratch=()):
    pairs = width // PAIR
    part = lambda at: ((rows, PAIR), lambda j, meta: (0, at * pairs + j), (rows, width))
    specs = {
        0: part(0),
        1: part(1),
        2: part(2),
        "row": ((1, 2, rows), lambda j, meta: (j, 0, 0), (pairs, 2, rows)),
        "mix": ((1, PAIR, rows), lambda j, meta: (j, 0, 0), (pairs, PAIR, rows)),
        "two": ((rows, 2 * width), lambda j, meta: (0, 0), (rows, 2 * width)),
        "three": ((rows, 3 * width), lambda j, meta: (0, 0), (rows, 3 * width)),
    }
    return pl.pallas_call(
        kernel,
        grid_spec=pltpu.PrefetchScalarGridSpec(
            num_scalar_prefetch=1,
            grid=(pairs,),
            in_specs=[pl.BlockSpec(*specs[kind][:2]) for kind, _ in operands],
            out_specs=[pl.BlockSpec(*specs[kind][:2]) for kind, _ in outs],
            scratch_shapes=list(scratch),
        ),
        out_shape=[jax.ShapeDtypeStruct(specs[kind][2], dtype) for kind, dtype in outs],
        cost_estimate=pl.CostEstimate(
            flops=8 * rows * rows * width, bytes_accessed=rows * width * 16,
            transcendentals=rows * rows * width // HDIM,
        ),
        name=name,
    )(meta, *(array for _, array in operands))


def attend(meta, width, near, far_kv):
    return attention_call(
        forward_kernel, "attend", meta, near.shape[0], width,
        [(0, near), (1, near), (2, near), (0, far_kv), (1, far_kv)],
        [(0, LOW), ("row", SINGLE)],
        [pltpu.VMEM((PAIR, near.shape[0]), SINGLE)],
    )


def attend_far_back(meta, width, near, far_kv, grads, attended, logs):
    rows = near.shape[0]
    return attention_call(
        far_backward_kernel, "attend_far_back", meta, rows, width,
        [(0, near), (0, far_kv), (1, far_kv), (0, grads), (0, attended), ("row", logs)],
        [("two", LOW), ("row", SINGLE), ("mix", SINGLE)],
        [pltpu.VMEM((2, rows, PAIR), SINGLE)],
    )


def attend_near_back(meta, width, near, grads, logs, inner, mixed):
    rows = near.shape[0]
    return attention_call(
        near_backward_kernel, "attend_near_back", meta, rows, width,
        [(0, near), (1, near), (2, near), (0, grads), ("row", logs), ("row", inner),
         ("mix", mixed)],
        [("three", LOW)],
        [pltpu.VMEM((2, rows, PAIR), SINGLE)],
    )[0]


def after(value, *gates):
    return lax.optimization_barrier((value, *gates))[0]


class Place:
    def __init__(self):
        self.n_shard = lax.axis_size("shard")
        self.n_ctx = lax.axis_size("ctx")
        self.n_tp = lax.axis_size("tp")
        self.shard = lax.axis_index("shard")
        self.ctx = lax.axis_index("ctx")
        self.half = self.ctx // 2
        self.core = self.ctx % 2
        self.tp = lax.axis_index("tp")
        self.home = self.core == self.tp // 2

    def core_swap(self, value):
        return lax.ppermute(value, "ctx", [(i, i ^ 1) for i in range(self.n_ctx)])

    def half_swap(self, value):
        return lax.ppermute(value, "ctx", [(i, i ^ 2) for i in range(self.n_ctx)])

    def half_up(self, value):
        return lax.ppermute(value, "ctx", [(0, 2), (1, 3)])

    def half_down(self, value):
        return lax.ppermute(value, "ctx", [(2, 0), (3, 1)])

    def shard_swap(self, value):
        return lax.ppermute(value, "shard", [(0, 1), (1, 0)])

    def tp_swap(self, value, mask):
        return lax.ppermute(value, "tp", [(i, i ^ mask) for i in range(self.n_tp)])

    def ordered(self, flag, mine, other, axis=0):
        first = jnp.where(flag == 0, mine, other)
        second = jnp.where(flag == 0, other, mine)
        return jnp.stack([first, second], axis)


    def own_block(self, piece, far):
        kept = jnp.where(self.home, piece, far)
        sent = jnp.where(self.home, far, piece)
        return self.ordered(self.core, kept, self.core_swap(sent)).reshape(-1, piece.shape[1])

    def over_shards(self, value):
        if self.n_shard == 2:
            return self.ordered(self.shard, value, self.shard_swap(value))
        return lax.all_gather(value, "shard", axis=0)

    def rows_half_first(self, block):
        value = self.over_shards(self.ordered(self.half, block, self.half_swap(block)))
        return value.reshape(-1, block.shape[1])

    def rows_shard_first(self, block):
        value = self.over_shards(block)
        value = self.ordered(self.half, value, self.half_swap(value), 1)
        return value.reshape(-1, block.shape[1])


    def split_rows(self, value):
        rows, width = value.shape
        return value.reshape(self.n_shard, 2, rows // (2 * self.n_shard), width)

    def step(self, values, index, axis, swap):
        pick = lambda value, at: lax.dynamic_index_in_dim(value, at, axis, False)
        sent = [pick(value, 1 - index).astype(LOW) for value in values]
        sent = jnp.concatenate(sent, -1) if len(sent) > 1 else sent[0]
        got, steps, start = swap(sent), [], 0
        for value in values:
            stop = start + value.shape[-1]
            steps.append((pick(value, index), got[..., start:stop], sent))
            start = stop
        return steps

    def half_steps(self, values, axis):
        return self.step(values, self.half, axis, self.half_swap)

    def half_step(self, value, axis):
        return self.half_steps([value], axis)[0]

    def shard_steps(self, values):
        if self.n_shard == 2:
            return self.step(values, self.shard, 0, self.shard_swap)
        kept = [
            lax.psum_scatter(value, "shard", scatter_dimension=0, tiled=False) for value in values
        ]
        return [(value, jnp.zeros_like(value, LOW), value) for value in kept]

    def shard_step(self, value):
        return self.shard_steps([value])[0]

    def block_step(self, value):
        pieces = value.reshape(2, -1, value.shape[1])
        sent = lax.dynamic_index_in_dim(pieces, 1 - self.core, 0, False).astype(LOW)
        kept = lax.dynamic_index_in_dim(pieces, self.core, 0, False)
        got = self.core_swap(sent).astype(SINGLE)
        sent = jnp.where(self.home, got, kept).astype(LOW)
        return jnp.where(self.home, kept, got), self.tp_swap(sent, 2), sent

    def tp_all(self, pair, arriving):
        value = self.ordered(self.tp % 2, pair, arriving, 1)
        return value.reshape(4, *pair.shape[1:])

    def chip_total(self, value):
        value = value + self.core_swap(value)
        value = value + self.half_swap(value)
        if self.n_shard == 2:
            return value + self.shard_swap(value)
        return lax.psum(value, "shard")


def added(step, *gates):
    kept, arriving = step[:2]
    return kept + after(arriving, *gates).astype(SINGLE)


def interleaved(first, second, width):
    parts = []
    for start in range(0, first.shape[1], width):
        parts += [first[:, start : start + width], second[:, start : start + width]]
    return jnp.concatenate(parts, 1)


def shards(
    tokens,
    lengths,
    first_gain,
    entry_weight,
    entry_bias,
    exit_weight,
    exit_bias,
    second_gain,
    hidden_weight,
    hidden_bias,
    return_weight,
    return_bias,
    cotangent,
):
    place = Place()
    local, narrow = tokens.shape[1:]
    part = entry_weight.shape[1]
    head_width = entry_weight.shape[2]
    units = hidden_weight.shape[1]

    width = 2 * head_width

    piece_a = jnp.concatenate([entry_weight[1], entry_weight[2], entry_weight[0], exit_weight.T], 1)
    piece_b = jnp.concatenate([hidden_weight, return_weight.T], 1)
    biases = jnp.concatenate([entry_bias.reshape(-1), hidden_bias])
    far_a = place.tp_swap(piece_a, 2)
    bias_far = place.tp_swap(biases, 2)
    bias_mine = jnp.where(place.home, biases, bias_far)
    bias_two = jnp.stack([bias_mine, place.tp_swap(bias_mine, 1)])
    bias_q = bias_two[:, :head_width].reshape(-1)
    bias_v = bias_two[:, head_width:width].reshape(-1)
    bias_h = bias_two[:, width:].reshape(-1)
    mine_a = place.own_block(piece_a, far_a)
    other_a = place.tp_swap(mine_a, 1)

    wide = narrow + 1
    sequence = after(place.tp, bias_far)
    length = lax.dynamic_index_in_dim(lengths, sequence, 0, False)
    meta = jnp.stack([place.half, place.core, length, place.ctx]).astype(jnp.int32)
    tokens_low = lax.dynamic_index_in_dim(tokens, sequence, 0, False)
    cot_low = lax.dynamic_index_in_dim(cotangent, after(sequence, tokens_low), 0, False)
    stream, first_unit, first_inverse, cot_full, normed_own, own_two = prepare(
        after(meta, mine_a), tokens_low, cot_low, first_gain.reshape(1, wide)
    )
    far_own = place.half_up(normed_own)
    all_two = jnp.concatenate([own_two, place.core_swap(own_two)], 0)
    first_normed, returned_grad = all_two[:, :wide], all_two[:, wide:]

    block_kv = interleaved(mine_a[:, :width], other_a[:, :width], head_width)
    block_qe = interleaved(mine_a[:, width:], other_a[:, width:], head_width)
    half_kv = place.ordered(place.half, block_kv, place.half_swap(block_kv))
    weight_kv = place.over_shards(half_kv).reshape(-1, 2 * width)
    weight_qe = place.rows_shard_first(block_qe)
    exit_t = weight_qe[:, width:]
    weight_all = jnp.concatenate([weight_qe[:, :width], weight_kv], 1)
    piece_b = after(piece_b, other_a)
    mine_b = place.own_block(piece_b, place.tp_swap(piece_b, 2))
    other_b = place.tp_swap(mine_b, 1)

    far_own = after(far_own, weight_kv)
    far_normed = jnp.concatenate([far_own, place.core_swap(far_own)], 0)
    bias_all = jnp.concatenate([bias_q, jnp.zeros_like(bias_v), bias_v])
    block_h = jnp.concatenate([mine_b[:, :units], other_b[:, :units]], 1)
    block_r = jnp.concatenate([mine_b[:, units:], other_b[:, units:]], 1)
    block_h, block_r = after((block_h, block_r), weight_kv, weight_qe)
    half_h = place.ordered(place.half, block_h, place.half_swap(block_h))
    shard_r = place.over_shards(block_r)
    if place.n_shard == 2:
        last_h = place.shard_swap(half_h)
        hidden_full = place.ordered(place.shard, half_h, last_h)
    else:
        last_h = hidden_full = lax.all_gather(half_h, "shard")
    hidden_full = hidden_full.reshape(-1, 2 * units)
    last_r = place.half_swap(shard_r)
    return_t = place.ordered(place.half, shard_r, last_r, 1)
    return_t = return_t.reshape(-1, 2 * units)
    near = (dot(after(first_normed, half_h), weight_all) + bias_all).astype(LOW)
    far_kv = (dot(after(far_normed, half_h), weight_kv) + bias_all[width:]).astype(LOW)
    attended, logs = attend(meta, width, near, after(far_kv, half_h, shard_r))

    def joined(product, left, weight):
        sent = product(left[local:], weight).astype(LOW)
        return product(left[:local], weight), place.core_swap(sent)

    branch = added(joined(dot_nt, attended, exit_t), last_h, last_r) + exit_bias
    middle = stream + branch - row_mean(branch)
    second_inverse = lax.rsqrt(row_mean(middle * middle) + EPSILON)
    second_unit = middle * second_inverse
    second_own = (second_unit * second_gain).astype(LOW)
    second_normed = jnp.concatenate([second_own, place.core_swap(second_own)], 0)
    hidden = dot(second_normed, hidden_full) + bias_h
    activated, gelu_pull = jax.vjp(
        lambda values_in: jax.nn.gelu(values_in, approximate=True), hidden
    )
    activated_low = activated.astype(LOW)
    hidden_grad = gelu_pull(dot(returned_grad, return_t))[0].astype(LOW)

    returned_step = joined(dot_nt, activated_low, return_t)
    second_step = joined(dot_nt, after(hidden_grad, returned_step[0]), hidden_full)
    returned = added(returned_step, second_step[0]) + return_bias
    full_stream = middle + returned - row_mean(returned)
    result_own = full_stream.astype(LOW)
    result_far = place.tp_swap(result_own, 2)
    second_grad = added(second_step, result_own)

    second_scaled = second_grad * second_gain
    middle_grad = cot_full + second_inverse * (
        second_scaled - second_unit * row_mean(second_scaled * second_unit)
    )
    branch_own = (middle_grad - row_mean(middle_grad)).astype(LOW)
    branch_other = place.core_swap(branch_own)

    hidden_weight_grad = dot_tn(after(second_normed, branch_own), hidden_grad)
    return_weight_grad = dot_tn(returned_grad, after(activated_low, branch_own))
    step_h = place.half_step(place.split_rows(hidden_weight_grad), 1)
    step_r = place.shard_step(place.split_rows(return_weight_grad))

    branch_other = after(branch_other, step_h[2], step_r[2])
    branch_grad = jnp.concatenate([branch_own, branch_other], 0)
    attended_grad = dot(branch_grad, exit_t).astype(LOW)
    far_dkv, inner, mixed = attend_far_back(
        meta, width, near, far_kv, attended_grad, attended, logs
    )
    far_step = joined(dot_nt, far_dkv, weight_kv)
    exit_weight_grad = dot_tn(after(branch_grad, far_step[0]), attended)
    far_sum = added(far_step, exit_weight_grad).astype(LOW)
    far_grad = place.half_down(far_sum)
    result_pair = place.ordered(place.tp // 2, result_own, after(result_far, exit_weight_grad))
    result_near = place.tp_swap(result_pair, 1)
    mixed = after(mixed, far_sum, result_pair)
    grads = attend_near_back(meta, width, near, attended_grad, logs, inner, mixed)
    sent = dot_nt(grads[local:], weight_all).astype(LOW)
    kept = dot_nt(grads[:local], weight_all)
    sent = after(sent, result_near, far_grad)
    step_h = place.shard_step(added(step_h, kept))
    step_r = place.half_step(added(step_r, kept), 0)
    first_grad = added((kept, place.core_swap(sent)), step_h[2], step_r[2]) + far_grad.astype(SINGLE)
    first_scaled = first_grad * first_gain
    stream_grad = middle_grad + first_inverse * (
        first_scaled - first_unit * row_mean(first_scaled * first_unit)
    )
    tokens_rows = (stream_grad - stream_grad[:, narrow:]).astype(LOW)
    tokens_far = place.tp_swap(tokens_rows, 2)

    normed_late = after(first_normed, tokens_rows)
    grads = after(grads, tokens_rows)
    query_weight_grad = dot_tn(normed_late, grads[:, :width])
    kv_weight_grad = dot_tn(normed_late, grads[:, width:]) + dot_tn(
        after(far_normed, tokens_rows), far_dkv
    )
    sum_h, sum_r = added(step_h, kv_weight_grad), added(step_r, kv_weight_grad)
    mlp_sent = jnp.concatenate([sum_h[:, units:], sum_r[:, units:]], 1).astype(LOW)
    mlp = (jnp.concatenate([sum_h[:, :units], sum_r[:, :units]], 1), place.tp_swap(mlp_sent, 1))
    step_q, step_e = place.shard_steps(
        [place.split_rows(query_weight_grad), place.split_rows(exit_weight_grad)]
    )
    step_kv = place.half_step(place.split_rows(kv_weight_grad), 1)
    tokens_pair = place.ordered(
        place.tp // 2, tokens_rows, after(tokens_far, step_kv[2], step_q[2])
    )
    tokens_near = place.tp_swap(tokens_pair, 1)
    result = place.tp_all(result_pair, after(result_near, tokens_pair))[:, :, :narrow]
    mlp = place.block_step(added(mlp, tokens_pair, result))
    mlp_first = mlp[2]
    step_q, step_e = place.half_steps(
        [added(step_q, mlp_first), added(step_e, mlp_first)], 0
    )
    step_kv = place.shard_step(added(step_kv, mlp_first))
    sums, sum_kv = [added(step_q), added(step_e)], added(step_kv)
    sums += [sum_kv[:, :width], sum_kv[:, width:]]
    sums = [
        jnp.concatenate([value[:, low : low + head_width] for value in sums], 1)
        for low in (0, head_width)
    ]
    heads = place.tp_swap(after(sums[1].astype(LOW), mlp[1]), 1)
    heads = added((sums[0], heads), tokens_near)
    heads_sum = heads
    heads = place.block_step(heads)
    tokens_grad = place.tp_all(tokens_pair, after(tokens_near, heads[2]))[:, :, :narrow]
    mlp, heads = added(mlp, heads[0]), added(heads)
    at = lambda index: heads[:, index * head_width : (index + 1) * head_width]
    entry_grad = jnp.stack([at(0), at(2), at(3)])
    exit_grad = at(1).T
    hidden_out = mlp[:, :units]
    return_out = mlp[:, units:].T

    return_bias_grad = jnp.sum(own_two[:, wide:].astype(SINGLE), 0)
    exit_bias_grad = jnp.sum(branch_own.astype(SINGLE), 0)
    first_gain_grad = jnp.sum(first_grad * first_unit, 0)
    second_gain_grad = jnp.sum(second_grad * second_unit, 0)
    query_sum = jnp.sum(grads[:, :width].astype(SINGLE), 0).reshape(2, head_width)
    value_sum = jnp.sum(grads[:, 2 * width :].astype(SINGLE), 0)
    value_sum = (value_sum + jnp.sum(far_dkv[:, width:].astype(SINGLE), 0)).reshape(2, head_width)
    hidden_sum = jnp.sum(hidden_grad.astype(SINGLE), 0).reshape(2, units)
    blocks = jnp.concatenate([query_sum, value_sum, hidden_sum], 1)
    first_id = jnp.where(place.home, place.tp, place.tp ^ 2)
    slots = []
    for slot in range(4):
        slots.append(
            jnp.where(first_id == slot, blocks[0], 0.0)
            + jnp.where(first_id == (slot ^ 1), blocks[1], 0.0)
        )
    pieces = [first_gain_grad, exit_bias_grad, second_gain_grad, return_bias_grad] + slots
    pieces = after(pieces, tokens_pair, mlp_sent)
    vectors = place.chip_total(after(jnp.concatenate(pieces), mlp_first))
    vectors = vectors + after(place.tp_swap(vectors, 1), heads_sum)
    vectors = vectors + after(place.tp_swap(vectors, 2), heads[2])
    own = lax.dynamic_index_in_dim(vectors[4 * wide :].reshape(4, -1), place.tp, 0, False)
    return (
        result,
        tokens_grad,
        vectors[:wide],
        entry_grad,
        own[:width].reshape(2, head_width),
        exit_grad,
        vectors[wide : 2 * wide],
        vectors[2 * wide : 3 * wide],
        hidden_out,
        own[width:],
        return_out,
        vectors[3 * wide : 4 * wide],
    )


def solution(mesh):
    return jax.shard_map(
        shards,
        mesh=mesh,
        in_specs=(
            P("shard", "ctx", None),
            P("shard"),
            P(),
            P(None, ("shard", "ctx"), "tp"),
            P(None, "tp"),
            P("tp", ("shard", "ctx")),
            P(),
            P(),
            P(("shard", "ctx"), "tp"),
            P("tp"),
            P("tp", ("shard", "ctx")),
            P(),
            P("shard", "ctx", None),
        ),
        out_specs=(
            P("shard", "ctx", None),
            P("shard", "ctx", None),
            P(),
            P(None, ("shard", "ctx"), "tp"),
            P(None, "tp"),
            P("tp", ("shard", "ctx")),
            P(),
            P(),
            P(("shard", "ctx"), "tp"),
            P("tp"),
            P("tp", ("shard", "ctx")),
            P(),
        ),
        check_vma=False,
    )
```
